512 devices in a mesh: tile: 8 (over z), comp: 64 (over y, x, core).
Axes of the slice: x: 4, y: 8, z: 8, core: 2. Of those that a mesh axis runs over, the one named last changes fastest.
Arguments:
- spectrum: float32 [1152, 8, 8192], P('comp', 'tile'), may hold values from 0.05 to 2
- sea_mask: int32 [512, 256], P('tile'), may hold values from 0 to 1, as said below
- sea_order: int32 [8, 8192], P('tile'), may hold values from 0 to 16383, as said below
- depth_class: int32 [512, 256], P('tile'), may hold values from 0 to 7
- wind_speed: float32 [512, 256], P('tile'), may hold values from 2 to 20
- wind_angle: float32 [512, 256], P('tile'), may hold values from -3.140625 to 3.140625
- speed_table: float32 [8, 36], replicated, may hold values from 0.2 to 0.7
- friction_table: float32 [8, 36], replicated, may hold values from 0.05 to 0.5
Outputs:
- spectrum_out: float32 [1152, 8, 8192], P('comp', 'tile')
The draws below stay inside these ranges and needn't reach their ends.
Inputs may be any that keep to these rules, and one draw needn't show every extreme that they name: `sea_mask`: each grid row of a tile holds at most 128 sea cells and at least 64; in some tile every row holds exactly 128. `sea_order`: slots r * (128) to (r + 1) * 128 - 1 of a tile hold distinct cells of its local row r; that row's sea cells all appear there, before any land cell.
All inputs are finite; a program needn't handle non-finite values.
Results may differ from the reference program's by a relative error of at most 0.00009.
Values sent between devices are 32-bit elements; how exact they have to be, the bound alone decides.
A program may use at most 64 MiB of HBM per device.

```python
import math
import jax
import jax.numpy as jnp
from jax import lax

NF = 36
ND = 32
NDEPTH = 8
GX = 64
GY = 256
TILES = 8
SEA_CAP = 8192
NX = 512
NY = 256


def sea_layout(key):
    base = jax.random.fold_in(key, 11)
    count_key, pick_key, noise_key = jax.random.split(base, 3)
    half = GY // 2
    counts = jax.random.randint(count_key, (TILES, GX), half // 2, half + 1)
    chosen = jax.random.randint(pick_key, (), 0, TILES)
    counts = jnp.where(jnp.arange(TILES)[:, None] == chosen, half, counts)
    column = jnp.arange(GY, dtype=jnp.int32)
    noise = jax.random.randint(noise_key, (TILES, GX, GY), 0, 4 * GY)
    scores = (column[None, None, :] * 4 + noise) * GY + column[None, None, :]
    ordering = jnp.argsort(-scores, axis=2)
    ranks = jnp.argsort(ordering, axis=2)
    water = (ranks < counts[:, :, None]).astype(jnp.int32)
    row_base = (jnp.arange(GX, dtype=jnp.int32) * GY)[None, :, None]
    order = (ordering[:, :, :half].astype(jnp.int32) + row_base).reshape(TILES, SEA_CAP)
    return (order.astype(jnp.int32), water.reshape(TILES * GX, GY))


def draw_sea_mask(key, part):
    return sea_layout(key)[1]


def draw_sea_order(key, part):
    return sea_layout(key)[0]


def plant(array, own_key, smallest, top_value):
    shape = array.shape
    index_at = [jax.random.randint(jax.random.fold_in(own_key, axis), (), 0, shape[axis]) for axis in range(len(shape))]
    array = array.at[tuple(index_at)].set(smallest)
    longest = shape.index(max(shape))
    index_at[longest] = (index_at[longest] + 1) % shape[longest]
    return array.at[tuple(index_at)].set(top_value)


def block_scale(rng, extent, pieces, least, top_value):
    def one(position, blocks):
        draws = jax.random.uniform(jax.random.fold_in(jax.random.fold_in(rng, 6), position), (blocks,), jnp.float32, least / len(pieces), top_value / len(pieces))
        return jnp.repeat(jnp.exp(draws), extent[position] // blocks).reshape((-1,) + (1,) * (len(extent) - position - 1))

    gain = one(*pieces[0])
    for cut in pieces[1:]:
        gain = gain * one(*cut)
    return gain


def setup_inputs(seed: int = 0) -> dict:
    arg_keys = jax.random.split(jax.random.key(seed), 9)
    return {
        "spectrum": jnp.clip(jnp.exp(math.log(2.0) - 3.6888794 * jax.random.uniform(arg_keys[0], (NF * ND, TILES, SEA_CAP), jnp.float32) ** block_scale(arg_keys[0], (NF * ND, TILES, SEA_CAP), ((0, 64), (1, 8)), -0.2, 0.2)), 0.05, 2.0),
        "sea_mask": draw_sea_mask(jax.random.fold_in(arg_keys[8], 71), 0),
        "sea_order": draw_sea_order(jax.random.fold_in(arg_keys[8], 71), 0),
        "depth_class": plant(jax.random.randint(arg_keys[3], (NX, NY), 0, NDEPTH), jax.random.fold_in(arg_keys[3], 1), 0, NDEPTH - 1).astype(jnp.int32),
        "wind_speed": jnp.clip(2.0 + 18.0 * jax.random.uniform(arg_keys[4], (NX, NY), jnp.float32) ** block_scale(arg_keys[4], (NX, NY), ((0, 8),), -0.2, 0.2), 2.0, 20.0),
        "wind_angle": jnp.clip(jax.random.uniform(arg_keys[5], (NX, NY), jnp.float32, -3.140625, 3.140625), -3.140625, 3.140625),
        "speed_table": jnp.clip(jnp.exp(jax.random.uniform(arg_keys[6], (NDEPTH, NF), jnp.float32, math.log(0.2), math.log(0.7))), 0.2, 0.7),
        "friction_table": jnp.clip(jnp.exp(jax.random.uniform(arg_keys[7], (NDEPTH, NF), jnp.float32, math.log(0.05), math.log(0.5))), 0.05, 0.5),
    }


def wave_constants():
    theta = (jnp.arange(ND).astype(jnp.float32) + 0.5) * (2.0 * math.pi / ND)
    freq = 0.04 * jnp.exp(jnp.arange(NF).astype(jnp.float32) * (math.log(28.0) / (NF - 1)))
    return theta, freq


def donor_step(energy, along_x, along_y):
    plus_x = jnp.maximum(along_x, 0.0) * energy
    minus_x = jnp.minimum(along_x, 0.0) * energy
    plus_y = jnp.maximum(along_y, 0.0) * energy
    minus_y = jnp.minimum(along_y, 0.0) * energy
    from_low_x = jnp.pad(plus_x, ((0, 0), (1, 0), (0, 0)))[:, :-1, :]
    from_high_x = jnp.pad(minus_x, ((0, 0), (0, 1), (0, 0)))[:, 1:, :]
    from_low_y = jnp.pad(plus_y, ((0, 0), (0, 0), (1, 0)))[:, :, :-1]
    from_high_y = jnp.pad(minus_y, ((0, 0), (0, 0), (0, 1)))[:, :, 1:]
    outflow = (jnp.abs(along_x) + jnp.abs(along_y)) * energy
    return energy - outflow + from_low_x - from_high_x + from_low_y - from_high_y


def point_factors(first_moment, second_moment, water_slot):
    safe = jnp.where(water_slot > 0, first_moment, 1.0)
    mean_freq = jnp.where(water_slot > 0, second_moment / safe, 1.0)
    steep = first_moment * mean_freq ** 4
    return mean_freq, steep


def reference(spectrum, sea_mask, sea_order, depth_class, wind_speed, wind_angle, speed_table, friction_table):
    theta, freq = wave_constants()
    water = sea_mask.astype(jnp.float32)
    water_flat = water.reshape(-1)
    tile_base = (jnp.arange(TILES) * (GX * GY)).astype(jnp.int32)
    slot_cells = (sea_order + tile_base[:, None]).reshape(-1).astype(jnp.int32)
    speed_cells = jnp.transpose(speed_table[depth_class], (2, 0, 1))
    slots = spectrum.reshape(NF, ND, TILES * SEA_CAP)
    cosines = jnp.cos(theta)[:, None, None]
    sines = jnp.sin(theta)[:, None, None]

    def advect(pair):
        energy_slots, speed = pair
        field = jnp.zeros((ND, NX * NY), jnp.float32).at[:, slot_cells].set(energy_slots)
        field = (field * water_flat[None, :]).reshape(ND, NX, NY)
        speed_water = (speed * water)[None]
        moved = donor_step(field, cosines * speed_water, sines * speed_water) * water[None]
        return moved.reshape(ND, NX * NY)[:, slot_cells]

    moved = lax.map(advect, (slots, speed_cells))
    weight = 0.1 * freq * (2.0 * math.pi / ND)
    weight_freq = weight * freq
    first_moment = jnp.sum(moved * weight[:, None, None], axis=(0, 1))
    second_moment = jnp.sum(moved * weight_freq[:, None, None], axis=(0, 1))
    water_slot = water_flat[slot_cells]
    depth_slot = depth_class.reshape(-1)[slot_cells]
    wind_slot = wind_speed.reshape(-1)[slot_cells]
    angle_slot = wind_angle.reshape(-1)[slot_cells]
    mean_freq, steep = point_factors(first_moment, second_moment, water_slot)
    friction = jnp.transpose(friction_table[depth_slot], (1, 0))

    def apply(triple):
        energy, freq_one, friction_one = triple
        push = 0.05 * jnp.maximum(wind_slot[None, :] * freq_one * jnp.cos(theta[:, None] - angle_slot[None, :]) - 1.0, 0.0)
        damp = 2.0 * (freq_one / mean_freq)[None, :] * (steep * steep)[None, :]
        return water_slot[None, :] * energy * jnp.exp(push - damp - friction_one[None, :])

    result = lax.map(apply, (moved, freq, friction))
    return result.reshape(NF * ND, TILES, SEA_CAP)
```

```python
import functools
import math

import jax
import jax.numpy as jnp
import numpy as np
from jax import lax
from jax.experimental import pallas as pl
from jax.experimental.pallas import tpu as pltpu
from jax.sharding import PartitionSpec as P

NF = 36
ND = 32
LANES = 128
GROUP = 8
MESH = pl.DeviceIdType.MESH


def constants():
    theta = (np.arange(ND) + 0.5) * (2.0 * math.pi / ND)
    freq = 0.04 * np.exp(np.arange(NF) * (math.log(28.0) / (NF - 1)))
    weight = 0.1 * freq * (2.0 * math.pi / ND)
    return np.concatenate([np.cos(theta), np.sin(theta), freq, weight]).astype(np.float32)


def take(x, index):
    return jnp.take_along_axis(x, index, axis=1, mode="promise_in_bounds")


def take_wide(low, high, column):
    index = column & (LANES - 1)
    return jnp.where(column >= LANES, take(high, index), take(low, index))


def step_kernel(
    tiles, y_count,
    spectrum_hbm, order_hbm, mask_hbm, depth_hbm, wind_hbm, angle_hbm, speed_s, friction_s, const_s,
    p_ref, x_ref,
    e, order_v, mask_v, depth_v, wind_v, angle_v,
    col_v, water_v, inv, nbr, nbr_mask, spd, fri, wx, wy, g, edge, coef, halo_out, halo_in,
    part, part_in, total, total_in, damp_out, damp,
    in_sem, halo_send, halo_recv, a_send, a_recv, b_send, b_recv, c_send, c_recv,
):
    comps, rows, lanes = e.shape
    tile = lax.axis_index("tile")
    comp = lax.axis_index("comp")
    q = comp % GROUP
    y = comp // GROUP
    first = comp * comps
    f0 = first // ND
    f1 = (first + comps - 1) // ND
    after = (tile + 1) % tiles
    before = (tile + tiles - 1) % tiles

    copies = [
        pltpu.make_async_copy(src, dst, in_sem.at[i])
        for i, (src, dst) in enumerate(
            [(order_hbm, order_v), (mask_hbm, mask_v), (depth_hbm, depth_v), (spectrum_hbm, e),
             (wind_hbm, wind_v), (angle_hbm, angle_v)]
        )
    ]
    for copy in copies:
        copy.start()

    barrier = pltpu.get_barrier_semaphore()
    for o in range(1, GROUP):
        pl.semaphore_signal(barrier, inc=1, device_id=(tile, y * GROUP + (q + o) % GROUP), device_id_type=MESH)
    for o in range(1, y_count):
        pl.semaphore_signal(barrier, inc=1, device_id=(tile, (y + o) % y_count * GROUP + q), device_id_type=MESH)
    pl.semaphore_signal(barrier, inc=1, device_id=(after, comp), device_id_type=MESH)
    pl.semaphore_signal(barrier, inc=1, device_id=(before, comp), device_id_type=MESH)

    zero8 = jnp.zeros((8, lanes), jnp.float32)
    for k in range(comps):
        g[k, 0:8, :] = zero8
        g[k, rows + 8 : rows + 16, :] = zero8
    none8 = jnp.full((8, lanes), -1, jnp.int32)
    for h in range(2):
        inv[h, 0:8, :] = none8
        inv[h, rows + 8 : rows + 16, :] = none8

    copies[0].wait()
    copies[1].wait()
    lane = lax.broadcasted_iota(jnp.int32, (rows, lanes), 1)
    row = lax.broadcasted_iota(jnp.int32, (rows, lanes), 0)
    column = order_v[...] - row * (2 * lanes)
    col_v[...] = column
    water = take_wide(mask_v[:, :lanes], mask_v[:, lanes:], column)
    water_v[...] = water.astype(jnp.float32)
    wet = jnp.where(water > 0, column, 4 * lanes)
    inv[0, 8 : rows + 8, :] = wet
    unroll = 8

    def invert(i, carry):
        low, high = carry
        base = pltpu.roll(inv[0, 8 : rows + 8, :], i * unroll, 1)
        for j in range(unroll):
            turned = base if j == 0 else pltpu.roll(base, j, 1)
            slot = (lane - (i * unroll + j)) & (lanes - 1)
            low = jnp.where(turned == lane, slot, low)
            high = jnp.where(turned == lane + lanes, slot, high)
        return low, high

    none = jnp.full((rows, lanes), -1, jnp.int32)
    low, high = lax.fori_loop(0, lanes // unroll, invert, (none, none))
    inv[0, 8 : rows + 8, :] = low
    inv[1, 8 : rows + 8, :] = high

    water = water_v[...]

    def neighbour(where, found, valid):
        nbr[where] = jnp.maximum(found, 0)
        nbr_mask[where] = jnp.where(valid, water, 0.0)

    for b in range(2):
        found = take_wide(inv[0, 7 + 2 * b : 7 + 2 * b + rows, :], inv[1, 7 + 2 * b : 7 + 2 * b + rows, :], column)
        neighbour(b, found, found >= 0)
        shifted = column - 1 + 2 * b
        inside = (shifted >= 0) & (shifted < 2 * lanes)
        found = take_wide(low, high, shifted & (2 * lanes - 1))
        neighbour(2 + b, found, (found >= 0) & inside)

    copies[2].wait()
    depth = take_wide(depth_v[:, :lanes], depth_v[:, lanes:], column)
    for i, f in enumerate((f0, f1)):
        s = jnp.full((rows, lanes), speed_s[0, f])
        r = jnp.full((rows, lanes), friction_s[0, f])
        for n in range(1, 8):
            s = jnp.where(depth == n, speed_s[n, f], s)
            r = jnp.where(depth == n, friction_s[n, f], r)
        spd[i] = s * water
        fri[i] = r

    coef[...] = jnp.zeros_like(coef)
    copies[3].wait()

    def advect(k, carry):
        m0, m1 = carry
        f = (first + k) // ND
        d = (first + k) % ND
        i = f - f0
        bx = (d + 8) // 16 % 2
        by = d // 16
        cos = jnp.abs(const_s[d])
        sin = jnp.abs(const_s[ND + d])
        weight = const_s[2 * ND + NF + f]
        energy = e[k]
        flux = energy * spd[i]
        g[k, 8 : rows + 8, :] = flux
        gx = take(g[k, pl.ds(7 + 2 * bx, rows), :], nbr[bx])
        gy = take(flux, nbr[2 + by])
        moved = energy * water_v[...] - (cos + sin) * flux + cos * (nbr_mask[bx] * gx) + sin * (nbr_mask[2 + by] * gy)
        p_ref[k] = moved
        edge[0, pl.ds(k, 1), :] = flux[rows - 1 : rows]
        edge[1, pl.ds(k, 1), :] = flux[0:1]
        coef[bx * 2 + i, pl.ds(k, 1), :] = jnp.full((1, lanes), cos)
        return m0 + weight * moved, m1 + (weight * const_s[2 * ND + f]) * moved

    zero = jnp.zeros((rows, lanes), jnp.float32)
    m0, m1 = lax.fori_loop(0, comps, advect, (zero, zero))
    for n in range(GROUP):
        part[n, 0] = m0[8 * n : 8 * n + 8]
        part[n, 1] = m1[8 * n : 8 * n + 8]

    pad = edge.shape[1]
    for b, at in ((0, rows - 1), (1, 0)):
        for h in range(2):
            found = jnp.broadcast_to(inv[h, 8 + at : 9 + at, :], (pad, lanes))
            halo_out[b, h] = jnp.where(found >= 0, take(edge[b], jnp.maximum(found, 0)), 0.0)

    pl.semaphore_wait(barrier, GROUP - 1 + y_count - 1 + 2)

    halos = [
        pltpu.make_async_remote_copy(
            src_ref=halo_out.at[b], dst_ref=halo_in.at[b], send_sem=halo_send.at[b], recv_sem=halo_recv.at[b],
            device_id=(to, comp), device_id_type=MESH,
        )
        for b, to in ((0, after), (1, before))
    ]
    for copy in halos:
        copy.start()

    def scatter(n):
        return pltpu.make_async_remote_copy(
            src_ref=part.at[n], dst_ref=part_in.at[q], send_sem=a_send.at[n], recv_sem=a_recv.at[q],
            device_id=(tile, y * GROUP + n), device_id_type=MESH,
        )

    def send_part(n):
        @pl.when(q != n)
        def _():
            scatter(n).start()

    for n in range(1, GROUP - 1):
        send_part(n)

    copies[4].wait()
    copies[5].wait()
    wind = take_wide(wind_v[:, :lanes], wind_v[:, lanes:], column)
    angle = take_wide(angle_v[:, :lanes], angle_v[:, lanes:], column)
    wx[...] = 0.05 * wind * jnp.cos(angle)
    wy[...] = 0.05 * wind * jnp.sin(angle)

    for copy in halos:
        copy.wait()
    sub = lax.broadcasted_iota(jnp.int32, (8, lanes), 0)
    live = (
        ((tile + tiles - 1) // tiles).astype(jnp.float32),
        ((2 * tiles - 2 - tile) // tiles).astype(jnp.float32),
    )
    for b, at in ((0, 0), (1, rows - 1)):
        column1 = jnp.broadcast_to(col_v[at : at + 1, :], (pad, lanes))
        scale = water_v[at : at + 1, :] * live[b]
        came = take_wide(halo_in[b, 0], halo_in[b, 1], column1) * scale
        c0 = came * coef[2 * b]
        c1 = came * coef[2 * b + 1]
        edge[b] = c0 + c1
        s0 = jnp.sum(c0[:comps], axis=0, keepdims=True)
        s1 = jnp.sum(c1[:comps], axis=0, keepdims=True)
        w0 = const_s[2 * ND + NF + f0]
        w1 = const_s[2 * ND + NF + f1]
        d0 = w0 * s0 + w1 * s1
        d1 = (w0 * const_s[2 * ND + f0]) * s0 + (w1 * const_s[2 * ND + f1]) * s1
        n = at // 8
        here = sub == at % 8
        part[n, 0] += jnp.where(here, d0, 0.0)
        part[n, 1] += jnp.where(here, d1, 0.0)
        send_part(n)

    def boundary(k, carry):
        d = (first + k) % ND
        bx = (d + 8) // 16 % 2
        p_ref[k, pl.ds((rows - 1) * bx, 1), :] += edge[bx, pl.ds(k, 1), :]
        return carry

    lax.fori_loop(0, comps, boundary, 0)

    def sources(k, carry):
        f = (first + k) // ND
        d = (first + k) % ND
        freq = const_s[2 * ND + f]
        push = jnp.maximum((freq * const_s[d]) * wx[...] + (freq * const_s[ND + d]) * wy[...] - 0.05, 0.0)
        p_ref[k] = p_ref[k] * jnp.exp(push - fri[f - f0])
        return carry

    lax.fori_loop(0, comps, sources, 0)

    a0 = part[q, 0]
    a1 = part[q, 1]
    for o in range(1, GROUP):
        source = (q + GROUP - o) % GROUP
        pltpu.make_async_remote_copy(
            src_ref=part.at[o], dst_ref=part_in.at[source], send_sem=a_send.at[o], recv_sem=a_recv.at[source],
            device_id=(tile, y * GROUP + (q + o) % GROUP), device_id_type=MESH,
        ).wait_recv()
        a0 += part_in[source, 0]
        a1 += part_in[source, 1]
    total[0] = a0
    total[1] = a1

    exchanges = [
        pltpu.make_async_remote_copy(
            src_ref=total, dst_ref=total_in.at[y], send_sem=b_send.at[o], recv_sem=b_recv.at[y],
            device_id=(tile, (y + o) % y_count * GROUP + q), device_id_type=MESH,
        )
        for o in range(1, y_count)
    ]
    for copy in exchanges:
        copy.start()
    for o in range(1, y_count):
        source = (y + y_count - o) % y_count
        pltpu.make_async_remote_copy(
            src_ref=total, dst_ref=total_in.at[source], send_sem=b_send.at[o], recv_sem=b_recv.at[source],
            device_id=(tile, (y + o) % y_count * GROUP + q), device_id_type=MESH,
        ).wait_recv()
        a0 += total_in[source, 0]
        a1 += total_in[source, 1]

    wet_here = water_v[pl.ds(pl.multiple_of(q * 8, 8), 8), :] > 0
    mean = jnp.where(wet_here, a1 / jnp.where(wet_here, a0, 1.0), 1.0)
    square = mean * mean
    alpha = a0 * (square * square)
    mine = 2.0 * alpha * alpha / mean
    damp_out[...] = mine
    gathers = [
        pltpu.make_async_remote_copy(
            src_ref=damp_out, dst_ref=damp.at[q], send_sem=c_send.at[o], recv_sem=c_recv.at[q],
            device_id=(tile, y * GROUP + (q + o) % GROUP), device_id_type=MESH,
        )
        for o in range(1, GROUP)
    ]
    for copy in gathers:
        copy.start()
    damp[q] = mine
    for o in range(1, GROUP):
        source = (q + GROUP - o) % GROUP
        pltpu.make_async_remote_copy(
            src_ref=damp_out, dst_ref=damp.at[source], send_sem=c_send.at[o], recv_sem=c_recv.at[source],
            device_id=(tile, y * GROUP + (q + o) % GROUP), device_id_type=MESH,
        ).wait_recv()
    factor = damp[...].reshape(rows, lanes)
    x_ref[0] = jnp.exp(-const_s[2 * ND + f0] * factor)
    x_ref[1] = jnp.exp(-const_s[2 * ND + f1] * factor)

    for n in range(GROUP):
        @pl.when(q != n)
        def _():
            scatter(n).wait_send()
    for copy in exchanges:
        copy.wait_send()
    for copy in gathers:
        copy.wait_send()


def body(tiles, y_count, spectrum, sea_mask, sea_order, depth_class, wind_speed, wind_angle, speed_table, friction_table):
    comps = spectrum.shape[0]
    rows = sea_mask.shape[0]
    f32, i32 = jnp.float32, jnp.int32
    hbm = pl.BlockSpec(memory_space=pltpu.HBM)
    vmem = pl.BlockSpec(memory_space=pltpu.VMEM)
    smem = pl.BlockSpec(memory_space=pltpu.SMEM)
    grid = (rows, LANES)
    wide = (rows, 2 * LANES)
    pad = -(-comps // 8) * 8
    V, D = pltpu.VMEM, pltpu.SemaphoreType.DMA
    p, x = pl.pallas_call(
        functools.partial(step_kernel, tiles, y_count),
        out_shape=(jax.ShapeDtypeStruct((comps,) + grid, f32), jax.ShapeDtypeStruct((2,) + grid, f32)),
        in_specs=[hbm] * 6 + [smem] * 3,
        out_specs=(vmem, vmem),
        scratch_shapes=[
            V((comps,) + grid, f32), V(grid, i32), V(wide, i32), V(wide, i32), V(wide, f32), V(wide, f32),
            V(grid, i32), V(grid, f32), V((2, rows + 16, LANES), i32), V((4,) + grid, i32), V((4,) + grid, f32),
            V((2,) + grid, f32), V((2,) + grid, f32), V(grid, f32), V(grid, f32),
            V((comps, rows + 16, LANES), f32), V((2, pad, LANES), f32), V((4, pad, LANES), f32),
            V((2, 2, pad, LANES), f32), V((2, 2, pad, LANES), f32),
            V((GROUP, 2, 8, LANES), f32), V((GROUP, 2, 8, LANES), f32),
            V((2, 8, LANES), f32), V((y_count, 2, 8, LANES), f32),
            V((8, LANES), f32), V((GROUP, 8, LANES), f32),
            D((6,)), D((2,)), D((2,)), D((GROUP,)), D((GROUP,)), D((y_count,)), D((y_count,)), D((GROUP,)), D((GROUP,)),
        ],
        compiler_params=pltpu.CompilerParams(collective_id=0, has_side_effects=True, vmem_limit_bytes=32 << 20),
        name="wave_step",
    )(
        spectrum.reshape(comps, rows, LANES), sea_order.reshape(grid), sea_mask, depth_class, wind_speed, wind_angle,
        speed_table, friction_table, jnp.asarray(constants()),
    )
    first = lax.axis_index("comp") * comps
    second = (first + jnp.arange(comps)) // ND > first // ND
    result = p * jnp.where(second[:, None, None], x[1][None], x[0][None])
    return result.reshape(spectrum.shape)


def solution(mesh):
    return jax.shard_map(
        functools.partial(body, mesh.shape["tile"], mesh.shape["comp"] // GROUP),
        mesh=mesh,
        in_specs=(
            P("comp", "tile", None),
            P("tile", None),
            P("tile", None),
            P("tile", None),
            P("tile", None),
            P("tile", None),
            P(),
            P(),
        ),
        out_specs=P("comp", "tile", None),
        check_vma=False,
    )
```

```python
import functools
import math

import jax
import jax.numpy as jnp
import numpy as np
from jax import lax
from jax.experimental import pallas as pl
from jax.experimental.pallas import tpu as pltpu
from jax.sharding import PartitionSpec as P

NF = 36
ND = 32
LANES = 128
GROUP = 8
MESH = pl.DeviceIdType.MESH


def constants():
    theta = (np.arange(ND) + 0.5) * (2.0 * math.pi / ND)
    freq = 0.04 * np.exp(np.arange(NF) * (math.log(28.0) / (NF - 1)))
    weight = 0.1 * freq * (2.0 * math.pi / ND)
    return np.concatenate([np.cos(theta), np.sin(theta), freq, weight]).astype(np.float32)


def take(x, index):
    return jnp.take_along_axis(x, index, axis=1, mode="promise_in_bounds")


def take_wide(low, high, column):
    index = column & (LANES - 1)
    return jnp.where(column >= LANES, take(high, index), take(low, index))


def step_kernel(
    tiles, y_count,
    spectrum_hbm, order_hbm, mask_hbm, depth_hbm, wind_hbm, angle_hbm, speed_hbm, friction_hbm, const_hbm,
    p_ref, x_ref,
    speed_s, friction_s, const_s,
    e, order_v, mask_v, depth_v, wind_v, angle_v,
    col_v, water_v, inv, nbr, spd, sx, sy, fri, wx, wy, coef, halo_out, halo_in,
    part, part_in, total, total_in, damp_out, damp,
    in_sem, halo_send, halo_recv, a_send, a_recv, b_send, b_recv, c_send, c_recv,
):
    comps = e.shape[0]
    rows, lanes = order_v.shape
    tile = lax.axis_index("tile")
    comp = lax.axis_index("comp")
    q = comp % GROUP
    y = comp // GROUP
    first = comp * comps
    f0 = first // ND
    f1 = (first + comps - 1) // ND
    after = (tile + 1) % tiles
    before = (tile + tiles - 1) % tiles
    inner = slice(8, rows + 8)

    copies = [
        pltpu.make_async_copy(src, dst, in_sem.at[i])
        for i, (src, dst) in enumerate(
            [(order_hbm, order_v), (mask_hbm, mask_v), (depth_hbm, depth_v),
             (speed_hbm, speed_s), (friction_hbm, friction_s), (const_hbm, const_s),
             (spectrum_hbm, e.at[:, inner, :]), (wind_hbm, wind_v), (angle_hbm, angle_v)]
        )
    ]
    for copy in copies:
        copy.start()

    barrier = pltpu.get_barrier_semaphore()
    for o in range(1, y_count):
        pl.semaphore_signal(barrier, inc=1, device_id=(tile, (y + o) % y_count * GROUP + q), device_id_type=MESH)
    for o in range(1, GROUP):
        pl.semaphore_signal(barrier, inc=1, device_id=(tile, y * GROUP + (q + o) % GROUP), device_id_type=MESH)
    pl.semaphore_signal(barrier, inc=1, device_id=(after, comp), device_id_type=MESH)
    pl.semaphore_signal(barrier, inc=1, device_id=(before, comp), device_id_type=MESH)

    zero8 = jnp.zeros((8, lanes), jnp.float32)
    none8 = jnp.full((8, lanes), -1, jnp.int32)
    for pad in (slice(0, 8), slice(rows + 8, rows + 16)):
        for k in range(comps):
            e[k, pad, :] = zero8
        for h in range(2):
            inv[h, pad, :] = none8
            spd[h, pad, :] = zero8
    coef[...] = jnp.zeros_like(coef)

    for copy in copies[:5]:
        copy.wait()
    lane = lax.broadcasted_iota(jnp.int32, (rows, lanes), 1)
    row = lax.broadcasted_iota(jnp.int32, (rows, lanes), 0)
    column = order_v[...] - row * (2 * lanes)
    col_v[...] = column
    wet = take_wide(mask_v[:, :lanes], mask_v[:, lanes:], column) > 0
    water = jnp.where(wet, 1.0, 0.0)
    water_v[...] = water
    wet_column = jnp.where(wet, column, 4 * lanes)
    depth = take_wide(depth_v[:, :lanes], depth_v[:, lanes:], column)
    for i, f in enumerate((f0, f1)):
        s = jnp.full((rows, lanes), speed_s[0, f])
        r = jnp.full((rows, lanes), friction_s[0, f])
        for n in range(1, 8):
            s = jnp.where(depth == n, speed_s[n, f], s)
            r = jnp.where(depth == n, friction_s[n, f], r)
        spd[i, inner, :] = s * water
        fri[i] = r

    copies[5].wait()
    copies[6].wait()
    for b, at in ((0, rows - 1), (1, 0)):
        for k in range(comps):
            i = (first + k) // ND - f0
            halo_out[b, k : k + 1, :] = e[k, 8 + at : 9 + at, :] * spd[i, 8 + at : 9 + at, :]
        halo_out[b, comps : comps + 1, :] = wet_column[at : at + 1].astype(jnp.float32)

    pl.semaphore_wait(barrier, GROUP - 1 + y_count - 1 + 2)
    halos = [
        pltpu.make_async_remote_copy(
            src_ref=halo_out.at[b], dst_ref=halo_in.at[b], send_sem=halo_send.at[b], recv_sem=halo_recv.at[b],
            device_id=(to, comp), device_id_type=MESH,
        )
        for b, to in ((0, after), (1, before))
    ]
    for copy in halos:
        copy.start()

    low = jnp.full((rows, lanes), -1, jnp.int32)
    high = low
    far = lane + lanes
    for j in range(lanes):
        turned = wet_column if j == 0 else pltpu.roll(wet_column, j, 1)
        slot = (lane - j) & (lanes - 1)
        low = jnp.where(turned == lane, slot, low)
        high = jnp.where(turned == far, slot, high)
    inv[0, inner, :] = low
    inv[1, inner, :] = high

    for b in range(2):
        rows_at = slice(7 + 2 * b, 7 + 2 * b + rows)
        found = take_wide(inv[0, rows_at, :], inv[1, rows_at, :], column)
        index = jnp.maximum(found, 0)
        nbr[b] = index
        for i in range(2):
            sx[2 * i + b] = jnp.where(found >= 0, take(spd[i, rows_at, :], index), 0.0) * water
        shifted = column - 1 + 2 * b
        inside = (shifted >= 0) & (shifted < 2 * lanes)
        found = jnp.where(inside, take_wide(low, high, shifted & (2 * lanes - 1)), -1)
        index = jnp.maximum(found, 0)
        nbr[2 + b] = index
        for i in range(2):
            sy[2 * i + b] = jnp.where(found >= 0, take(spd[i, inner, :], index), 0.0) * water

    def advect_one(k, m0, m1):
        f = (first + k) // ND
        d = (first + k) % ND
        i = f - f0
        bx = (d + 8) // 16 % 2
        by = d // 16
        cos = jnp.abs(const_s[d])
        sin = jnp.abs(const_s[ND + d])
        weight = const_s[2 * ND + NF + f]
        energy = e[k, inner, :]
        gx = take(e[k, pl.ds(7 + 2 * bx, rows), :], nbr[bx])
        gy = take(energy, nbr[2 + by])
        moved = energy * (water_v[...] - (cos + sin) * spd[i, inner, :])
        moved = moved + cos * (sx[2 * i + bx] * gx) + sin * (sy[2 * i + by] * gy)
        p_ref[k] = moved
        coef[bx * 2 + i, pl.ds(k, 1), :] = jnp.full((1, lanes), cos)
        return m0 + weight * moved, m1 + (weight * const_s[2 * ND + f]) * moved

    unroll = 3

    def advect(step, carry):
        m0, m1 = carry
        for u in range(unroll):
            m0, m1 = advect_one(step * unroll + u, m0, m1)
        return m0, m1

    zero = jnp.zeros((rows, lanes), jnp.float32)
    m0, m1 = lax.fori_loop(0, comps // unroll, advect, (zero, zero))
    for n in range(GROUP):
        part[n, 0] = m0[8 * n : 8 * n + 8]
        part[n, 1] = m1[8 * n : 8 * n + 8]

    def scatter(n):
        return pltpu.make_async_remote_copy(
            src_ref=part.at[n], dst_ref=part_in.at[q], send_sem=a_send.at[n], recv_sem=a_recv.at[q],
            device_id=(tile, y * GROUP + n), device_id_type=MESH,
        )

    def send_part(n):
        @pl.when(q != n)
        def _():
            scatter(n).start()

    for n in range(1, GROUP - 1):
        send_part(n)

    for copy in halos:
        copy.wait()
    sub = lax.broadcasted_iota(jnp.int32, (8, lanes), 0)
    lane8 = lane[:8]
    their = jnp.where(
        sub == 0, halo_in[0, comps : comps + 1, :], halo_in[1, comps : comps + 1, :]
    )
    ours = jnp.where(sub == 0, col_v[0:1, :], col_v[rows - 1 : rows, :]).astype(jnp.float32)
    match = jnp.full((8, lanes), -1, jnp.int32)
    for j in range(lanes):
        turned = their if j == 0 else pltpu.roll(their, j, 1)
        match = jnp.where(turned == ours, (lane8 - j) & (lanes - 1), match)
    live = (
        ((tile + tiles - 1) // tiles).astype(jnp.float32),
        ((2 * tiles - 2 - tile) // tiles).astype(jnp.float32),
    )
    pad = halo_in.shape[1]
    for b, at in ((0, 0), (1, rows - 1)):
        found = jnp.broadcast_to(match[b : b + 1], (pad, lanes))
        scale = water_v[at : at + 1, :] * live[b]
        came = jnp.where(found >= 0, take(halo_in[b], jnp.maximum(found, 0)), 0.0) * scale
        c0 = came * coef[2 * b]
        c1 = came * coef[2 * b + 1]
        halo_out[b] = c0 + c1
        s0 = jnp.sum(c0[:comps], axis=0, keepdims=True)
        s1 = jnp.sum(c1[:comps], axis=0, keepdims=True)
        w0 = const_s[2 * ND + NF + f0]
        w1 = const_s[2 * ND + NF + f1]
        d0 = w0 * s0 + w1 * s1
        d1 = (w0 * const_s[2 * ND + f0]) * s0 + (w1 * const_s[2 * ND + f1]) * s1
        n = at // 8
        here = sub == at % 8
        part[n, 0] += jnp.where(here, d0, 0.0)
        part[n, 1] += jnp.where(here, d1, 0.0)
        send_part(n)

    copies[7].wait()
    copies[8].wait()
    wind = take_wide(wind_v[:, :lanes], wind_v[:, lanes:], column)
    angle = take_wide(angle_v[:, :lanes], angle_v[:, lanes:], column)
    wx[...] = 0.05 * wind * jnp.cos(angle)
    wy[...] = 0.05 * wind * jnp.sin(angle)

    for k in range(comps):
        bx = ((first + k) % ND + 8) // 16 % 2
        p_ref[k, pl.ds((rows - 1) * bx, 1), :] += halo_out[bx, k : k + 1, :]

    def sources(step, carry):
        for u in range(unroll):
            k = step * unroll + u
            f = (first + k) // ND
            d = (first + k) % ND
            freq = const_s[2 * ND + f]
            push = jnp.maximum((freq * const_s[d]) * wx[...] + (freq * const_s[ND + d]) * wy[...] - 0.05, 0.0)
            p_ref[k] = p_ref[k] * jnp.exp(push - fri[f - f0])
        return carry

    lax.fori_loop(0, comps // unroll, sources, 0)

    a0 = part[q, 0]
    a1 = part[q, 1]
    for o in range(1, GROUP):
        source = (q + GROUP - o) % GROUP
        pltpu.make_async_remote_copy(
            src_ref=part.at[o], dst_ref=part_in.at[source], send_sem=a_send.at[o], recv_sem=a_recv.at[source],
            device_id=(tile, y * GROUP + (q + o) % GROUP), device_id_type=MESH,
        ).wait_recv()
        a0 += part_in[source, 0]
        a1 += part_in[source, 1]
    total[0] = a0
    total[1] = a1

    exchanges = [
        pltpu.make_async_remote_copy(
            src_ref=total, dst_ref=total_in.at[y], send_sem=b_send.at[o], recv_sem=b_recv.at[y],
            device_id=(tile, (y + o) % y_count * GROUP + q), device_id_type=MESH,
        )
        for o in range(1, y_count)
    ]
    for copy in exchanges:
        copy.start()
    for o in range(1, y_count):
        source = (y + y_count - o) % y_count
        pltpu.make_async_remote_copy(
            src_ref=total, dst_ref=total_in.at[source], send_sem=b_send.at[o], recv_sem=b_recv.at[source],
            device_id=(tile, (y + o) % y_count * GROUP + q), device_id_type=MESH,
        ).wait_recv()
        a0 += total_in[source, 0]
        a1 += total_in[source, 1]

    wet_here = water_v[pl.ds(pl.multiple_of(q * 8, 8), 8), :] > 0
    mean = jnp.where(wet_here, a1 / jnp.where(wet_here, a0, 1.0), 1.0)
    square = mean * mean
    alpha = a0 * (square * square)
    mine = 2.0 * alpha * alpha / mean
    damp_out[...] = mine
    gathers = [
        pltpu.make_async_remote_copy(
            src_ref=damp_out, dst_ref=damp.at[q], send_sem=c_send.at[o], recv_sem=c_recv.at[q],
            device_id=(tile, y * GROUP + (q + o) % GROUP), device_id_type=MESH,
        )
        for o in range(1, GROUP)
    ]
    for copy in gathers:
        copy.start()
    damp[q] = mine
    for o in range(1, GROUP):
        source = (q + GROUP - o) % GROUP
        pltpu.make_async_remote_copy(
            src_ref=damp_out, dst_ref=damp.at[source], send_sem=c_send.at[o], recv_sem=c_recv.at[source],
            device_id=(tile, y * GROUP + (q + o) % GROUP), device_id_type=MESH,
        ).wait_recv()
    factor = damp[...].reshape(rows, lanes)
    x_ref[0] = jnp.exp(-const_s[2 * ND + f0] * factor)
    x_ref[1] = jnp.exp(-const_s[2 * ND + f1] * factor)

    for n in range(GROUP):
        @pl.when(q != n)
        def _():
            scatter(n).wait_send()
    for copy in exchanges:
        copy.wait_send()
    for copy in gathers:
        copy.wait_send()


def body(tiles, y_count, spectrum, sea_mask, sea_order, depth_class, wind_speed, wind_angle, speed_table, friction_table):
    comps = spectrum.shape[0]
    rows = sea_mask.shape[0]
    f32, i32 = jnp.float32, jnp.int32
    hbm = pl.BlockSpec(memory_space=pltpu.HBM)
    vmem = pl.BlockSpec(memory_space=pltpu.VMEM)
    grid = (rows, LANES)
    wide = (rows, 2 * LANES)
    pad = -(-(comps + 1) // 8) * 8
    V, S, D = pltpu.VMEM, pltpu.SMEM, pltpu.SemaphoreType.DMA
    table = jnp.asarray(constants())
    operands = (
        spectrum.reshape(comps, rows, LANES), sea_order.reshape(grid), sea_mask, depth_class, wind_speed, wind_angle,
        speed_table, friction_table, table,
    )
    p, x = pl.pallas_call(
        functools.partial(step_kernel, tiles, y_count),
        out_shape=(jax.ShapeDtypeStruct((comps,) + grid, f32), jax.ShapeDtypeStruct((2,) + grid, f32)),
        in_specs=[hbm] * 9,
        out_specs=(vmem, vmem),
        scratch_shapes=[
            S(speed_table.shape, f32), S(friction_table.shape, f32), S(table.shape, f32),
            V((comps, rows + 16, LANES), f32), V(grid, i32), V(wide, i32), V(wide, i32), V(wide, f32), V(wide, f32),
            V(grid, i32), V(grid, f32), V((2, rows + 16, LANES), i32), V((4,) + grid, i32),
            V((2, rows + 16, LANES), f32), V((4,) + grid, f32), V((4,) + grid, f32), V((2,) + grid, f32),
            V(grid, f32), V(grid, f32), V((4, pad, LANES), f32), V((2, pad, LANES), f32), V((2, pad, LANES), f32),
            V((GROUP, 2, 8, LANES), f32), V((GROUP, 2, 8, LANES), f32),
            V((2, 8, LANES), f32), V((y_count, 2, 8, LANES), f32),
            V((8, LANES), f32), V((GROUP, 8, LANES), f32),
            D((9,)), D((2,)), D((2,)), D((GROUP,)), D((GROUP,)), D((y_count,)), D((y_count,)), D((GROUP,)), D((GROUP,)),
        ],
        compiler_params=pltpu.CompilerParams(collective_id=0, has_side_effects=True, vmem_limit_bytes=32 << 20),
        name="wave_step",
    )(*[pltpu.with_memory_space_constraint(z, pltpu.HBM) for z in operands])
    first = lax.axis_index("comp") * comps
    second = (first + jnp.arange(comps)) // ND > first // ND
    result = p * jnp.where(second[:, None, None], x[1][None], x[0][None])
    return result.reshape(spectrum.shape)


def solution(mesh):
    return jax.shard_map(
        functools.partial(body, mesh.shape["tile"], mesh.shape["comp"] // GROUP),
        mesh=mesh,
        in_specs=(
            P("comp", "tile", None),
            P("tile", None),
            P("tile", None),
            P("tile", None),
            P("tile", None),
            P("tile", None),
            P(),
            P(),
        ),
        out_specs=P("comp", "tile", None),
        check_vma=False,
    )
```

```python
import functools
import math

import jax
import jax.numpy as jnp
import numpy as np
from jax import lax
from jax.experimental import pallas as pl
from jax.experimental.pallas import tpu as pltpu
from jax.sharding import PartitionSpec as P

NF = 36
ND = 32
LANES = 128
GROUP = 8
MESH = pl.DeviceIdType.MESH


def constants():
    theta = (np.arange(ND) + 0.5) * (2.0 * math.pi / ND)
    freq = 0.04 * np.exp(np.arange(NF) * (math.log(28.0) / (NF - 1)))
    weight = 0.1 * freq * (2.0 * math.pi / ND)
    return np.concatenate([np.cos(theta), np.sin(theta), freq, weight]).astype(np.float32)


def take(x, index):
    return jnp.take_along_axis(x, index, axis=1, mode="promise_in_bounds")


def take_wide(low, high, column):
    index = column & (LANES - 1)
    return jnp.where(column >= LANES, take(high, index), take(low, index))


def step_kernel(
    tiles, y_count,
    spectrum_hbm, order_hbm, mask_hbm, depth_hbm, wind_hbm, angle_hbm, speed_hbm, friction_hbm, const_hbm,
    p_ref, x_ref,
    speed_s, friction_s, const_s,
    e, order_v, mask_v, depth_v, wind_v, angle_v,
    col_v, water_v, inv, nbr, spd, sx, sy, fri, wx, wy, edge, coef, halo_out, halo_in, rim_out, rim_in,
    part, part_in, total, total_in, damp_out, damp,
    in_sem, halo_send, halo_recv, rim_send, rim_recv, a_send, a_recv, b_send, b_recv, c_send, c_recv,
):
    comps = e.shape[0]
    rows, lanes = order_v.shape
    tile = lax.axis_index("tile")
    comp = lax.axis_index("comp")
    q = lax.rem(comp, GROUP)
    y = lax.div(comp, GROUP)
    first = comp * comps
    f0 = lax.div(first, ND)
    f1 = lax.div(first + comps - 1, ND)
    has = (tile < tiles - 1, tile > 0)
    beside = (tile + 1, tile - 1)
    owner = (y * GROUP, y * GROUP + GROUP - 1)
    group = [(tile, y * GROUP + lax.rem(q + o, GROUP)) for o in range(GROUP)]
    ring = [(tile, lax.rem(y + o, y_count) * GROUP + q) for o in range(y_count)]
    order_a = sorted(range(1, GROUP), key=lambda o: abs(2 * o - GROUP))
    order_b = sorted(range(1, y_count), key=lambda o: abs(2 * o - y_count))
    inner = slice(8, rows + 8)

    copies = [
        pltpu.make_async_copy(src, dst, in_sem.at[i])
        for i, (src, dst) in enumerate(
            [(order_hbm, order_v), (mask_hbm, mask_v), (depth_hbm, depth_v),
             (speed_hbm, speed_s), (friction_hbm, friction_s), (const_hbm, const_s),
             (spectrum_hbm, e.at[:, inner, :]), (wind_hbm, wind_v), (angle_hbm, angle_v)]
        )
    ]
    for copy in copies:
        copy.start()

    barrier = pltpu.get_barrier_semaphore()
    for to in [ring[o] for o in order_b] + [group[o] for o in order_a]:
        pl.semaphore_signal(barrier, inc=1, device_id=to, device_id_type=MESH)
    for b in range(2):
        @pl.when(has[b])
        def _():
            pl.semaphore_signal(barrier, inc=1, device_id=(beside[b], comp), device_id_type=MESH)

            @pl.when(comp == owner[1 - b])
            def _():
                for n in range(GROUP):
                    pl.semaphore_signal(barrier, inc=1, device_id=(beside[b], y * GROUP + n), device_id_type=MESH)

    zero8 = jnp.zeros((8, lanes), jnp.float32)
    none8 = jnp.full((8, lanes), -1, jnp.int32)
    for pad in (slice(0, 8), slice(rows + 8, rows + 16)):
        for k in range(comps):
            e[k, pad, :] = zero8
        for h in range(2):
            inv[h, pad, :] = none8
            spd[h, pad, :] = zero8
    coef[...] = jnp.zeros_like(coef)

    for copy in copies[:5]:
        copy.wait()
    lane = lax.broadcasted_iota(jnp.int32, (rows, lanes), 1)
    row = lax.broadcasted_iota(jnp.int32, (rows, lanes), 0)
    column = order_v[...] - row * (2 * lanes)
    col_v[...] = column
    wet = take_wide(mask_v[:, :lanes], mask_v[:, lanes:], column) > 0
    water = jnp.where(wet, 1.0, 0.0)
    water_v[...] = water
    wet_column = jnp.where(wet, column, 4 * lanes)
    depth = take_wide(depth_v[:, :lanes], depth_v[:, lanes:], column)
    for i, f in enumerate((f0, f1)):
        s = jnp.full((rows, lanes), speed_s[0, f])
        r = jnp.full((rows, lanes), friction_s[0, f])
        for n in range(1, 8):
            s = jnp.where(depth == n, speed_s[n, f], s)
            r = jnp.where(depth == n, friction_s[n, f], r)
        spd[i, inner, :] = s * water
        fri[i] = r

    copies[5].wait()
    copies[6].wait()
    for k in range(comps):
        i = lax.div(first + k, ND) - f0
        d = lax.rem(first + k, ND)
        bx = lax.rem(lax.div(d + 8, 16), 2)
        coef[2 * bx + i, k : k + 1, :] = jnp.full((1, lanes), jnp.abs(const_s[d]))
        for b, at in ((0, rows - 1), (1, 0)):
            edge[b, k : k + 1, :] = e[k, 8 + at : 9 + at, :] * spd[i, 8 + at : 9 + at, :]

    low = jnp.full((rows, lanes), -1, jnp.int32)
    high = low
    far = lane + lanes
    for j in range(lanes):
        turned = wet_column if j == 0 else pltpu.roll(wet_column, j, 1)
        slot = (lane - j) & (lanes - 1)
        low = jnp.where(turned == lane, slot, low)
        high = jnp.where(turned == far, slot, high)
    inv[0, inner, :] = low
    inv[1, inner, :] = high

    for b in range(2):
        rows_at = slice(7 + 2 * b, 7 + 2 * b + rows)
        found = take_wide(inv[0, rows_at, :], inv[1, rows_at, :], column)
        index = jnp.maximum(found, 0)
        nbr[b] = index
        for i in range(2):
            sx[2 * i + b] = jnp.where(found >= 0, take(spd[i, rows_at, :], index), 0.0) * water
        shifted = column - 1 + 2 * b
        inside = (shifted >= 0) & (shifted < 2 * lanes)
        found = jnp.where(inside, take_wide(low, high, shifted & (2 * lanes - 1)), -1)
        index = jnp.maximum(found, 0)
        nbr[2 + b] = index
        for i in range(2):
            sy[2 * i + b] = jnp.where(found >= 0, take(spd[i, inner, :], index), 0.0) * water

    sub = lax.broadcasted_iota(jnp.int32, (8, lanes), 0)
    pad = edge.shape[1]
    w0 = const_s[2 * ND + NF + f0]
    w1 = const_s[2 * ND + NF + f1]
    v0 = w0 * const_s[2 * ND + f0]
    v1 = w1 * const_s[2 * ND + f1]
    for b, at in ((0, rows - 1), (1, 0)):
        near = [inv[h, 8 + at : 9 + at, :] for h in range(2)]
        for h in range(2):
            found = jnp.broadcast_to(near[h], (pad, lanes))
            halo_out[b, h] = jnp.where(found >= 0, take(edge[b], jnp.maximum(found, 0)), 0.0)
        s0 = jnp.sum((edge[b] * coef[2 * b])[:comps], axis=0, keepdims=True)
        s1 = jnp.sum((edge[b] * coef[2 * b + 1])[:comps], axis=0, keepdims=True)
        both = jnp.where(lax.rem(sub, 2) == 0, w0 * s0 + w1 * s1, v0 * s0 + v1 * s1)
        found = jnp.where(sub < 2, near[0], near[1])
        rim_out[b] = jnp.where(found >= 0, take(both, jnp.maximum(found, 0)), 0.0)

    def halo(b, to):
        return pltpu.make_async_remote_copy(
            src_ref=halo_out.at[b], dst_ref=halo_in.at[b], send_sem=halo_send.at[b], recv_sem=halo_recv.at[b],
            device_id=(to, comp), device_id_type=MESH,
        )

    def rim(b):
        return pltpu.make_async_remote_copy(
            src_ref=rim_out.at[b], dst_ref=rim_in.at[q], send_sem=rim_send.at[b], recv_sem=rim_recv.at[q],
            device_id=(beside[b], owner[b]), device_id_type=MESH,
        )

    def announce():
        sides = lax.div(tile + tiles - 1, tiles) + lax.div(2 * tiles - 2 - tile, tiles)
        pl.semaphore_wait(barrier, GROUP - 1 + y_count - 1 + 2 * sides)
        for b in range(2):
            @pl.when(has[b])
            def _():
                rim(b).start()
                halo(b, beside[b]).start()

    late = jnp.abs(2 * y - y_count) <= 2
    pl.when(late)(announce)

    def advect_one(k, m0, m1):
        f = lax.div(first + k, ND)
        d = lax.rem(first + k, ND)
        i = f - f0
        bx = lax.rem(lax.div(d + 8, 16), 2)
        by = lax.div(d, 16)
        cos = jnp.abs(const_s[d])
        sin = jnp.abs(const_s[ND + d])
        weight = const_s[2 * ND + NF + f]
        energy = e[k, inner, :]
        gx = take(e[k, pl.ds(7 + 2 * bx, rows), :], nbr[bx])
        gy = take(energy, nbr[2 + by])
        moved = energy * (water_v[...] - (cos + sin) * spd[i, inner, :])
        moved = moved + cos * (sx[2 * i + bx] * gx) + sin * (sy[2 * i + by] * gy)
        p_ref[k] = moved
        return m0 + weight * moved, m1 + (weight * const_s[2 * ND + f]) * moved

    unroll = 3

    def advect(step, carry):
        m0, m1 = carry
        for u in range(unroll):
            m0, m1 = advect_one(step * unroll + u, m0, m1)
        return m0, m1

    zero = jnp.zeros((rows, lanes), jnp.float32)
    m0, m1 = lax.fori_loop(0, comps // unroll, advect, (zero, zero))
    for n in range(GROUP):
        part[n, 0] = m0[8 * n : 8 * n + 8]
        part[n, 1] = m1[8 * n : 8 * n + 8]

    pl.when(jnp.logical_not(late))(announce)

    scatters = {
        o: pltpu.make_async_remote_copy(
            src_ref=part.at[lax.rem(q + o, GROUP)], dst_ref=part_in.at[o], send_sem=a_send.at[o], recv_sem=a_recv.at[o],
            device_id=group[o], device_id_type=MESH,
        )
        for o in order_a
    }
    for o in order_a:
        scatters[o].start()

    copies[7].wait()
    copies[8].wait()
    wind = take_wide(wind_v[:, :lanes], wind_v[:, lanes:], column)
    angle = take_wide(angle_v[:, :lanes], angle_v[:, lanes:], column)
    wx[...] = 0.05 * wind * jnp.cos(angle)
    wy[...] = 0.05 * wind * jnp.sin(angle)

    a0 = part[q, 0]
    a1 = part[q, 1]
    for o in reversed(order_a):
        scatters[o].wait_recv()
        a0 += part_in[o, 0]
        a1 += part_in[o, 1]
    total[0] = a0
    total[1] = a1
    for b, n, at in ((0, 0, 0), (1, GROUP - 1, rows - 1)):
        @pl.when(jnp.logical_and(has[1 - b], q == n))
        def _():
            came = jnp.zeros((8, lanes), jnp.float32)
            for source in range(GROUP):
                pltpu.make_async_remote_copy(
                    src_ref=rim_out.at[b], dst_ref=rim_in.at[source], send_sem=rim_send.at[b], recv_sem=rim_recv.at[source],
                    device_id=(beside[1 - b], owner[b]), device_id_type=MESH,
                ).wait_recv()
                came += rim_in[source]
            column1 = col_v[at : at + 1, :]
            found = take(came, jnp.broadcast_to(column1 & (lanes - 1), (8, lanes)))
            far_side = column1 >= lanes
            ours = water_v[at : at + 1, :]
            here = sub == at % 8
            total[0] += jnp.where(here, jnp.where(far_side, found[2:3], found[0:1]) * ours, 0.0)
            total[1] += jnp.where(here, jnp.where(far_side, found[3:4], found[1:2]) * ours, 0.0)

    exchanges = {
        o: pltpu.make_async_remote_copy(
            src_ref=total, dst_ref=total_in.at[o], send_sem=b_send.at[o], recv_sem=b_recv.at[o],
            device_id=ring[o], device_id_type=MESH,
        )
        for o in order_b
    }
    for o in order_b:
        exchanges[o].start()

    for b, at in ((0, 0), (1, rows - 1)):
        @pl.when(has[1 - b])
        def _():
            halo(b, beside[1 - b]).wait_recv()
            column1 = jnp.broadcast_to(col_v[at : at + 1, :], (pad, lanes))
            came = take_wide(halo_in[b, 0], halo_in[b, 1], column1) * water_v[at : at + 1, :]
            came = came * (coef[2 * b] + coef[2 * b + 1])
            for k in range(comps):
                p_ref[k, at : at + 1, :] += came[k : k + 1]

    def sources(step, carry):
        for u in range(unroll):
            k = step * unroll + u
            f = lax.div(first + k, ND)
            d = lax.rem(first + k, ND)
            freq = const_s[2 * ND + f]
            push = jnp.maximum((freq * const_s[d]) * wx[...] + (freq * const_s[ND + d]) * wy[...] - 0.05, 0.0)
            p_ref[k] = p_ref[k] * jnp.exp(push - fri[f - f0])
        return carry

    lax.fori_loop(0, comps // unroll, sources, 0)

    a0 = total[0]
    a1 = total[1]
    for o in reversed(order_b):
        exchanges[o].wait_recv()
        a0 += total_in[o, 0]
        a1 += total_in[o, 1]

    wet_here = water_v[pl.ds(pl.multiple_of(q * 8, 8), 8), :] > 0
    mean = jnp.where(wet_here, a1 / jnp.where(wet_here, a0, 1.0), 1.0)
    square = mean * mean
    alpha = a0 * (square * square)
    mine = 2.0 * alpha * alpha / mean
    damp_out[...] = mine
    gathers = {
        o: pltpu.make_async_remote_copy(
            src_ref=damp_out, dst_ref=damp.at[q], send_sem=c_send.at[o], recv_sem=c_recv.at[o],
            device_id=group[o], device_id_type=MESH,
        )
        for o in order_a
    }
    for o in order_a:
        gathers[o].start()
    damp[q] = mine
    for o in reversed(order_a):
        source = lax.rem(q + GROUP - o, GROUP)
        pltpu.make_async_remote_copy(
            src_ref=damp_out, dst_ref=damp.at[source], send_sem=c_send.at[o], recv_sem=c_recv.at[o],
            device_id=group[o], device_id_type=MESH,
        ).wait_recv()
    factor = damp[...].reshape(rows, lanes)
    x_ref[0] = jnp.exp(-const_s[2 * ND + f0] * factor)
    x_ref[1] = jnp.exp(-const_s[2 * ND + f1] * factor)

    for copy in [*scatters.values(), *exchanges.values(), *gathers.values()]:
        copy.wait_send()
    for b in range(2):
        @pl.when(has[b])
        def _():
            rim(b).wait_send()
            halo(b, beside[b]).wait_send()


def body(tiles, y_count, spectrum, sea_mask, sea_order, depth_class, wind_speed, wind_angle, speed_table, friction_table):
    comps = spectrum.shape[0]
    rows = sea_mask.shape[0]
    f32, i32 = jnp.float32, jnp.int32
    hbm = pl.BlockSpec(memory_space=pltpu.HBM)
    vmem = pl.BlockSpec(memory_space=pltpu.VMEM)
    grid = (rows, LANES)
    wide = (rows, 2 * LANES)
    pad = -(-comps // 8) * 8
    V, S, D = pltpu.VMEM, pltpu.SMEM, pltpu.SemaphoreType.DMA
    table = jnp.asarray(constants())
    operands = (
        spectrum.reshape(comps, rows, LANES), sea_order.reshape(grid), sea_mask, depth_class, wind_speed, wind_angle,
        speed_table, friction_table, table,
    )
    p, x = pl.pallas_call(
        functools.partial(step_kernel, tiles, y_count),
        out_shape=(jax.ShapeDtypeStruct((comps,) + grid, f32), jax.ShapeDtypeStruct((2,) + grid, f32)),
        in_specs=[hbm] * 9,
        out_specs=(vmem, vmem),
        scratch_shapes=[
            S(speed_table.shape, f32), S(friction_table.shape, f32), S(table.shape, f32),
            V((comps, rows + 16, LANES), f32), V(grid, i32), V(wide, i32), V(wide, i32), V(wide, f32), V(wide, f32),
            V(grid, i32), V(grid, f32), V((2, rows + 16, LANES), i32), V((4,) + grid, i32),
            V((2, rows + 16, LANES), f32), V((4,) + grid, f32), V((4,) + grid, f32), V((2,) + grid, f32),
            V(grid, f32), V(grid, f32), V((2, pad, LANES), f32), V((4, pad, LANES), f32),
            V((2, 2, pad, LANES), f32), V((2, 2, pad, LANES), f32), V((2, 8, LANES), f32), V((GROUP, 8, LANES), f32),
            V((GROUP, 2, 8, LANES), f32), V((GROUP, 2, 8, LANES), f32),
            V((2, 8, LANES), f32), V((y_count, 2, 8, LANES), f32),
            V((8, LANES), f32), V((GROUP, 8, LANES), f32),
            D((9,)), D((2,)), D((2,)), D((2,)), D((GROUP,)), D((GROUP,)), D((GROUP,)), D((y_count,)), D((y_count,)), D((GROUP,)), D((GROUP,)),
        ],
        compiler_params=pltpu.CompilerParams(collective_id=0, has_side_effects=True, vmem_limit_bytes=32 << 20),
        name="wave_step",
    )(*[pltpu.with_memory_space_constraint(z, pltpu.HBM) for z in operands])
    first = lax.axis_index("comp") * comps
    second = (first + jnp.arange(comps)) // ND > first // ND
    result = p * jnp.where(second[:, None, None], x[1][None], x[0][None])
    return result.reshape(spectrum.shape)


def solution(mesh):
    return jax.shard_map(
        functools.partial(body, mesh.shape["tile"], mesh.shape["comp"] // GROUP),
        mesh=mesh,
        in_specs=(
            P("comp", "tile", None),
            P("tile", None),
            P("tile", None),
            P("tile", None),
            P("tile", None),
            P("tile", None),
            P(),
            P(),
        ),
        out_specs=P("comp", "tile", None),
        check_vma=False,
    )
```

```python
import functools
import math

import jax
import jax.numpy as jnp
import numpy as np
from jax import lax
from jax.experimental import pallas as pl
from jax.experimental.pallas import tpu as pltpu
from jax.sharding import PartitionSpec as P

NF = 36
ND = 32
LANES = 128
GROUP = 8
MESH = pl.DeviceIdType.MESH


def constants():
    theta = (np.arange(ND) + 0.5) * (2.0 * math.pi / ND)
    freq = 0.04 * np.exp(np.arange(NF) * (math.log(28.0) / (NF - 1)))
    weight = 0.1 * freq * (2.0 * math.pi / ND)
    return np.concatenate([np.cos(theta), np.sin(theta), freq, weight]).astype(np.float32)


def take(x, index):
    return lax.gather(
        x, index[..., None],
        lax.GatherDimensionNumbers((), (1,), (1,), (0,), (0,)),
        (1, 1), mode=lax.GatherScatterMode.PROMISE_IN_BOUNDS,
    )


def take_wide(low, high, column):
    index = column & (LANES - 1)
    return jnp.where(column >= LANES, take(high, index), take(low, index))


def step_kernel(
    tiles, y_count,
    spectrum_hbm, order_hbm, mask_hbm, depth_hbm, wind_hbm, angle_hbm, speed_hbm, friction_hbm, const_hbm, cos_hbm,
    p_ref, x_ref,
    speed_s, friction_s, const_s,
    cos_v, e, order_v, mask_v, depth_v, wind_v, angle_v,
    col_v, water_v, wet_v, inv, nbr, nbr_mask, spd, fri, wx, wy, edge, coef, halo_out, halo_in, rim_out, rim_in, rim_sum, rim_all,
    part, part_in, total, total_in, damp_out, damp,
    ready, in_sem, halo_send, halo_recv, rim_send, rim_recv, r_send, r_recv, a_send, a_recv, b_send, b_recv, c_send, c_recv,
):
    comps = e.shape[0]
    rows, lanes = order_v.shape
    tile = lax.axis_index("tile")
    comp = lax.axis_index("comp")
    q = lax.rem(comp, GROUP)
    y = lax.div(comp, GROUP)
    first = comp * comps
    f0 = lax.div(first, ND)
    f1 = lax.div(first + comps - 1, ND)
    has = (tile < tiles - 1, tile > 0)
    beside = (tile + 1, tile - 1)
    group = [(tile, y * GROUP + lax.rem(q + o, GROUP)) for o in range(GROUP)]
    ring = [(tile, lax.rem(y + o, y_count) * GROUP + q) for o in range(y_count)]
    order_a = sorted(range(1, GROUP), key=lambda o: abs(2 * o - GROUP))
    order_b = sorted(range(1, y_count), key=lambda o: abs(2 * o - y_count))
    inner = slice(8, rows + 8)

    copies = [
        pltpu.make_async_copy(src, dst, in_sem.at[i])
        for i, (src, dst) in enumerate(
            [(order_hbm, order_v), (mask_hbm, mask_v), (depth_hbm, depth_v),
             (wind_hbm, wind_v), (angle_hbm, angle_v), (speed_hbm, speed_s), (friction_hbm, friction_s),
             (const_hbm, const_s), (spectrum_hbm, e.at[:, inner, :]), (cos_hbm, cos_v)]
        )
    ]
    for copy in copies:
        copy.start()

    barrier = pltpu.get_barrier_semaphore()
    for to in [ring[o] for o in order_b] + [group[o] for o in order_a]:
        pl.semaphore_signal(barrier, inc=1, device_id=to, device_id_type=MESH)
    @pl.when(has[0])
    def _():
        for n in range(GROUP):
            pl.semaphore_signal(barrier, inc=1, device_id=(beside[0], y * GROUP + n), device_id_type=MESH)

    zero8 = jnp.zeros((8, lanes), jnp.float32)
    none8 = jnp.full((8, lanes), -1, jnp.int32)
    for pad in (slice(0, 8), slice(rows + 8, rows + 16)):
        for k in range(comps):
            e[k, pad, :] = zero8
        for h in range(2):
            inv[h, pad, :] = none8
            spd[h, pad, :] = zero8

    for copy in copies[:8]:
        copy.wait()
    copies[9].wait()
    sub = lax.broadcasted_iota(jnp.int32, (8, lanes), 0)
    spot = lax.broadcasted_iota(jnp.int32, (8, lanes), 1)
    groups = [slice(8 * n, 8 * n + 8) for n in range(GROUP)]
    inners = [slice(8 * n + 8, 8 * n + 16) for n in range(GROUP)]
    classes = [
        [(speed_s[n, f], friction_s[n, f]) for n in range(8)] for f in (f0, f1)
    ]
    for n, at in enumerate(groups):
        column = order_v[at, :] - (sub + 8 * n) * (2 * lanes)
        index = column & (lanes - 1)
        upper = column >= lanes
        cell = [
            jnp.where(upper, take(v[at, lanes:], index), take(v[at, :lanes], index))
            for v in (mask_v, depth_v, wind_v, angle_v)
        ]
        wet = cell[0] > 0
        water = jnp.where(wet, 1.0, 0.0)
        col_v[at, :] = column
        water_v[at, :] = water
        wet_v[at, :] = jnp.where(wet, column, 4 * lanes)
        wx[at, :] = cell[2]
        wy[at, :] = cell[3]
        s = [jnp.full((8, lanes), c[0][0]) for c in classes]
        r = [jnp.full((8, lanes), c[0][1]) for c in classes]
        for m in range(1, 8):
            here = cell[1] == m
            for i in range(2):
                s[i] = jnp.where(here, classes[i][m][0], s[i])
                r[i] = jnp.where(here, classes[i][m][1], r[i])
        for i in range(2):
            spd[i, inners[n], :] = s[i] * water
            fri[i, at, :] = r[i]

    narrow = jnp.int16
    lane = lax.broadcasted_iota(jnp.int32, (rows, lanes), 1)
    near = lane.astype(narrow)
    far = (lane + lanes).astype(narrow)
    here = wet_v[...].astype(narrow)
    low = jnp.full((rows, lanes), -1, narrow)
    high = low
    for j in range(lanes):
        turned = here if j == 0 else pltpu.roll(here, j, 1)
        slot = ((lane - j) & (lanes - 1)).astype(narrow)
        low = jnp.where(turned == near, slot, low)
        high = jnp.where(turned == far, slot, high)
    inv[0, inner, :] = low.astype(jnp.int32)
    inv[1, inner, :] = high.astype(jnp.int32)

    for n, at in enumerate(groups):
        column = col_v[at, :]
        water = water_v[at, :]
        index = column & (lanes - 1)
        upper = column >= lanes
        for b in range(2):
            rows_at = slice(8 * n + 7 + 2 * b, 8 * n + 15 + 2 * b)
            found = jnp.where(upper, take(inv[1, rows_at, :], index), take(inv[0, rows_at, :], index))
            nbr[b, at, :] = jnp.maximum(found, 0)
            nbr_mask[b, at, :] = jnp.where(found >= 0, water, 0.0)
        for b in range(2):
            shifted = column - 1 + 2 * b
            index = shifted & (lanes - 1)
            found = jnp.where(shifted >= lanes, take(inv[1, inners[n], :], index), take(inv[0, inners[n], :], index))
            inside = (shifted >= 0) & (shifted < 2 * lanes) & (found >= 0)
            nbr[2 + b, at, :] = jnp.maximum(found, 0)
            nbr_mask[2 + b, at, :] = jnp.where(inside, water, 0.0)

    copies[8].wait()
    pad = edge.shape[1]
    comp_at = first + lax.broadcasted_iota(jnp.int32, (pad, lanes), 0)
    second = comp_at >= ND * (f0 + 1)
    turn = (((comp_at & (ND - 1)) + 8) >> 4) & 1
    spread = jnp.abs(cos_v[pl.ds(lax.rem(first, ND), pad), :])
    for b in range(2):
        for i in range(2):
            coef[2 * b + i] = jnp.where((turn == b) & (second == (i == 1)), spread, 0.0)
    for b, at in ((0, rows - 1), (1, 0)):
        speed = jnp.where(second, spd[1, 8 + at : 9 + at, :], spd[0, 8 + at : 9 + at, :])
        edge[b, :comps, :] = e[:, 8 + at, :] * speed[:comps]

    w0 = const_s[2 * ND + NF + f0]
    w1 = const_s[2 * ND + NF + f1]
    v0 = w0 * const_s[2 * ND + f0]
    v1 = w1 * const_s[2 * ND + f1]
    for b, at in ((0, rows - 1), (1, 0)):
        back = [inv[h, 8 + at : 9 + at, :] for h in range(2)]
        for h in range(2):
            found = jnp.broadcast_to(back[h], (pad, lanes))
            halo_out[b, h] = jnp.where(found >= 0, take(edge[b], jnp.maximum(found, 0)), 0.0)
        s0 = jnp.sum((edge[b] * coef[2 * b])[:comps], axis=0, keepdims=True)
        s1 = jnp.sum((edge[b] * coef[2 * b + 1])[:comps], axis=0, keepdims=True)
        both = jnp.where(lax.rem(sub, 2) == 0, w0 * s0 + w1 * s1, v0 * s0 + v1 * s1)
        found = jnp.where(sub < 2, back[0], back[1])
        rim_out[b] = jnp.where(found >= 0, take(both, jnp.maximum(found, 0)), 0.0)

    def halo(b, to):
        return pltpu.make_async_remote_copy(
            src_ref=halo_out.at[b], dst_ref=halo_in.at[b], send_sem=halo_send.at[b], recv_sem=halo_recv.at[b],
            device_id=(to, comp), device_id_type=MESH,
        )

    def rim(b, n):
        return pltpu.make_async_remote_copy(
            src_ref=rim_out.at[b], dst_ref=rim_in.at[b, q], send_sem=rim_send.at[b], recv_sem=rim_recv.at[b],
            device_id=(beside[b], y * GROUP + n), device_id_type=MESH,
        )

    def drain(ref, sem):
        pltpu.make_async_copy(ref, ref, sem).wait()

    def send_beside(b):
        for n in (3, 4, 2, 5, 1, 6, 0, 7):
            rim(b, n).start()
        halo(b, beside[b]).start()

    def announce():
        pl.semaphore_wait(barrier, GROUP - 1 + y_count - 1 + GROUP * lax.div(tile + tiles - 1, tiles))

        @pl.when(has[1])
        def _():
            for n in range(GROUP):
                pl.semaphore_signal(ready, inc=1, device_id=(beside[1], y * GROUP + n), device_id_type=MESH)
            send_beside(1)

    late = jnp.abs(2 * y - y_count) <= 2
    pl.when(late)(announce)

    def advect(step, carry):
        sums = list(carry)
        for pair in range(3):
            advect_pair(6 * step + 2 * pair, sums)
        return tuple(sums)

    def advect_pair(k, sums):
        f = lax.div(first + k, ND)
        d = lax.rem(first + k, ND)
        i = f - f0
        bx = lax.rem(lax.div(d + 8, 16), 2)
        by = lax.div(d, 16)
        weight = const_s[2 * ND + NF + f]
        weight_freq = weight * const_s[2 * ND + f]
        cos = [jnp.abs(const_s[d + u]) for u in range(2)]
        sin = [jnp.abs(const_s[ND + d + u]) for u in range(2)]
        for n, at in enumerate(groups):
            speed = spd[i, inners[n], :]
            behind = pl.ds(8 * n + 7 + 2 * bx, 8)
            speed_x = spd[i, behind, :]
            energy = [e[k + u, inners[n], :] for u in range(2)]
            flux = [energy[u] * speed for u in range(2)]
            flux_x = [e[k + u, behind, :] * speed_x for u in range(2)]
            index = nbr[bx, at, :]
            gx = [take(flux_x[u], index) for u in range(2)]
            index = nbr[2 + by, at, :]
            gy = [take(flux[u], index) for u in range(2)]
            mask_x = nbr_mask[bx, at, :]
            mask_y = nbr_mask[2 + by, at, :]
            water = water_v[at, :]
            for u in range(2):
                moved = energy[u] * water - (cos[u] + sin[u]) * flux[u]
                moved = moved + cos[u] * (mask_x * gx[u]) + sin[u] * (mask_y * gy[u])
                p_ref[k + u, at, :] = moved
                sums[n] = sums[n] + weight * moved
                sums[GROUP + n] = sums[GROUP + n] + weight_freq * moved

    zero = jnp.zeros((8, lanes), jnp.float32)
    sums = lax.fori_loop(0, comps // 6, advect, (zero,) * (2 * GROUP))
    for n in range(GROUP):
        part[n, 0] = sums[n]
        part[n, 1] = sums[GROUP + n]

    pl.when(jnp.logical_not(late))(announce)

    scatters = {
        o: pltpu.make_async_remote_copy(
            src_ref=part.at[lax.rem(q + o, GROUP)], dst_ref=part_in.at[o - 1], send_sem=a_send, recv_sem=a_recv,
            device_id=group[o], device_id_type=MESH,
        )
        for o in order_a
    }
    for o in order_a:
        scatters[o].start()

    wind = 0.05 * wx[...]
    angle = wy[...]
    wx[...] = wind * jnp.cos(angle)
    wy[...] = wind * jnp.sin(angle)

    drain(part_in, a_recv)
    for h in range(2):
        held = part[q, h]
        for n in range(GROUP - 1):
            held += part_in[n, h]
        total[h] = held

    exchanges = {
        o: pltpu.make_async_remote_copy(
            src_ref=total, dst_ref=total_in.at[o - 1], send_sem=b_send, recv_sem=b_recv,
            device_id=ring[o], device_id_type=MESH,
        )
        for o in order_b
    }
    for o in order_b:
        exchanges[o].start()

    @pl.when(has[0])
    def _():
        pl.semaphore_wait(ready, GROUP)
        send_beside(0)

    for b, at in ((0, 0), (1, rows - 1)):
        @pl.when(has[1 - b])
        def _():
            halo(b, beside[1 - b]).wait_recv()
            column1 = jnp.broadcast_to(col_v[at : at + 1, :], (pad, lanes))
            came = take_wide(halo_in[b, 0], halo_in[b, 1], column1) * water_v[at : at + 1, :]
            came = came * (coef[2 * b] + coef[2 * b + 1])
            for k in range(comps):
                p_ref[k, at : at + 1, :] += came[k : k + 1]

    def sources(step, carry):
        for u in range(3):
            k = step * 3 + u
            f = lax.div(first + k, ND)
            d = lax.rem(first + k, ND)
            freq = const_s[2 * ND + f]
            push = jnp.maximum((freq * const_s[d]) * wx[...] + (freq * const_s[ND + d]) * wy[...] - 0.05, 0.0)
            p_ref[k] = p_ref[k] * jnp.exp(push - fri[f - f0])
        return carry

    lax.fori_loop(0, comps // 3, sources, 0)

    for b in range(2):
        rim_sum[b] = jnp.zeros((8, lanes), jnp.float32)

        @pl.when(has[1 - b])
        def _():
            drain(rim_in.at[b], rim_recv.at[b])
            came = rim_in[b, 0]
            for n in range(1, GROUP):
                came += rim_in[b, n]
            rim_sum[b] = came

    rims = {
        o: pltpu.make_async_remote_copy(
            src_ref=rim_sum, dst_ref=rim_all.at[o - 1], send_sem=r_send, recv_sem=r_recv,
            device_id=ring[o], device_id_type=MESH,
        )
        for o in order_b
    }
    for o in order_b:
        rims[o].start()

    drain(total_in, b_recv)
    a0 = total[0]
    a1 = total[1]
    for n in range(y_count - 1):
        a0 += total_in[n, 0]
        a1 += total_in[n, 1]

    def damping(m0, m1, wet):
        mean = jnp.where(wet, m1 / jnp.where(wet, m0, 1.0), 1.0)
        square = mean * mean
        alpha = m0 * (square * square)
        return 2.0 * alpha * alpha / mean

    outer = lax.div(q, GROUP - 1)
    rim0 = jnp.where(outer == 1, a0[7:8], a0[0:1])
    rim1 = jnp.where(outer == 1, a1[7:8], a1[0:1])
    wet_here = water_v[pl.ds(pl.multiple_of(q * 8, 8), 8), :] > 0
    mine = damping(a0, a1, wet_here)
    damp_out[0] = mine
    damp_out[1] = jnp.where(sub == 0, rim0, rim1)
    gathers = {
        o: pltpu.make_async_remote_copy(
            src_ref=damp_out, dst_ref=damp.at[q], send_sem=c_send, recv_sem=c_recv,
            device_id=group[o], device_id_type=MESH,
        )
        for o in order_a
    }
    for o in order_a:
        gathers[o].start()
    damp[q, 0] = mine
    damp[q, 1] = damp_out[1]
    drain(rim_all, r_recv)
    added = []
    for b, at in ((0, 0), (1, rows - 1)):
        came = rim_sum[b]
        for n in range(y_count - 1):
            came += rim_all[n, b]
        column1 = col_v[at : at + 1, :]
        found = take(came, jnp.broadcast_to(column1 & (lanes - 1), (8, lanes)))
        ours = water_v[at : at + 1, :]
        added.append(jnp.where(column1 >= lanes, found[2:4], found[0:2]) * ours)
    drain(damp.at[pl.ds(0, GROUP - 1)], c_recv)
    factor = [damp[n, 0] for n in range(GROUP)]
    for b, n, at in ((0, 0, 0), (1, GROUP - 1, rows - 1)):
        both = damp[n, 1][0:2] + added[b]
        fixed = damping(both[0:1], both[1:2], water_v[at : at + 1, :] > 0)
        factor[n] = jnp.where(sub == at % 8, fixed, factor[n])
    for n, at in enumerate(groups):
        x_ref[0, at, :] = jnp.exp(-const_s[2 * ND + f0] * factor[n])
        x_ref[1, at, :] = jnp.exp(-const_s[2 * ND + f1] * factor[n])

    drain(part_in, a_send)
    drain(total_in, b_send)
    drain(rim_all, r_send)
    drain(damp.at[pl.ds(0, GROUP - 1)], c_send)
    for b in range(2):
        @pl.when(has[b])
        def _():
            drain(rim_in.at[b], rim_send.at[b])
            halo(b, beside[b]).wait_send()


def body(tiles, y_count, spectrum, sea_mask, sea_order, depth_class, wind_speed, wind_angle, speed_table, friction_table):
    comps = spectrum.shape[0]
    rows = sea_mask.shape[0]
    f32, i32 = jnp.float32, jnp.int32
    hbm = pl.BlockSpec(memory_space=pltpu.HBM)
    vmem = pl.BlockSpec(memory_space=pltpu.VMEM)
    grid = (rows, LANES)
    wide = (rows, 2 * LANES)
    pad = -(-comps // 8) * 8
    V, S, D = pltpu.VMEM, pltpu.SMEM, pltpu.SemaphoreType.DMA
    numbers = constants()
    table = jnp.asarray(numbers)
    doubled = jnp.asarray(np.ascontiguousarray(np.broadcast_to(np.tile(numbers[:ND], 2)[:, None], (2 * ND, LANES))))
    operands = (
        spectrum.reshape(comps, rows, LANES), sea_order.reshape(grid), sea_mask, depth_class, wind_speed, wind_angle,
        speed_table, friction_table, table, doubled,
    )
    p, x = pl.pallas_call(
        functools.partial(step_kernel, tiles, y_count),
        out_shape=(jax.ShapeDtypeStruct((comps,) + grid, f32), jax.ShapeDtypeStruct((2,) + grid, f32)),
        in_specs=[hbm] * 10,
        out_specs=(vmem, vmem),
        scratch_shapes=[
            S(speed_table.shape, f32), S(friction_table.shape, f32), S(table.shape, f32),
            V(doubled.shape, f32), V((comps, rows + 16, LANES), f32),
            V(grid, i32), V(wide, i32), V(wide, i32), V(wide, f32), V(wide, f32),
            V(grid, i32), V(grid, f32), V(grid, i32), V((2, rows + 16, LANES), i32), V((4,) + grid, i32), V((4,) + grid, f32),
            V((2, rows + 16, LANES), f32), V((2,) + grid, f32),
            V(grid, f32), V(grid, f32), V((2, pad, LANES), f32), V((4, pad, LANES), f32),
            V((2, 2, pad, LANES), f32), V((2, 2, pad, LANES), f32), V((2, 8, LANES), f32), V((2, GROUP, 8, LANES), f32),
            V((2, 8, LANES), f32), V((y_count - 1, 2, 8, LANES), f32),
            V((GROUP, 2, 8, LANES), f32), V((GROUP - 1, 2, 8, LANES), f32),
            V((2, 8, LANES), f32), V((y_count - 1, 2, 8, LANES), f32),
            V((2, 8, LANES), f32), V((GROUP, 2, 8, LANES), f32),
            pltpu.SemaphoreType.REGULAR, D((10,)), D((2,)), D((2,)), D((2,)), D((2,)), D, D, D, D, D, D, D, D,
        ],
        compiler_params=pltpu.CompilerParams(collective_id=0, has_side_effects=True, vmem_limit_bytes=32 << 20),
        name="wave_step",
    )(*[pltpu.with_memory_space_constraint(z, pltpu.HBM) for z in operands])
    first = lax.axis_index("comp") * comps
    second = (first + jnp.arange(comps)) // ND > first // ND
    result = p * jnp.where(second[:, None, None], x[1][None], x[0][None])
    return result.reshape(spectrum.shape)


def solution(mesh):
    return jax.shard_map(
        functools.partial(body, mesh.shape["tile"], mesh.shape["comp"] // GROUP),
        mesh=mesh,
        in_specs=(
            P("comp", "tile", None),
            P("tile", None),
            P("tile", None),
            P("tile", None),
            P("tile", None),
            P("tile", None),
            P(),
            P(),
        ),
        out_specs=P("comp", "tile", None),
        check_vma=False,
    )
```

```python
import functools
import math

import jax
import jax.numpy as jnp
import numpy as np
from jax import lax
from jax.experimental import pallas as pl
from jax.experimental.pallas import tpu as pltpu
from jax.sharding import PartitionSpec as P

NF = 36
ND = 32
LANES = 128
GROUP = 8
MESH = pl.DeviceIdType.MESH


def constants():
    theta = (np.arange(ND) + 0.5) * (2.0 * math.pi / ND)
    freq = 0.04 * np.exp(np.arange(NF) * (math.log(28.0) / (NF - 1)))
    weight = 0.1 * freq * (2.0 * math.pi / ND)
    return np.concatenate([np.cos(theta), np.sin(theta), freq, weight]).astype(np.float32)


def take(x, index):
    return lax.gather(
        x, index[..., None],
        lax.GatherDimensionNumbers((), (1,), (1,), (0,), (0,)),
        (1, 1), mode=lax.GatherScatterMode.PROMISE_IN_BOUNDS,
    )


def take_wide(low, high, column):
    index = column & (LANES - 1)
    return jnp.where(column >= LANES, take(high, index), take(low, index))


def step_kernel(
    tiles, y_count,
    spectrum_hbm, order_hbm, mask_hbm, depth_hbm, wind_hbm, angle_hbm, speed_hbm, friction_hbm, const_hbm, cos_hbm,
    x_ref, p_ref,
    speed_s, friction_s, const_s,
    cos_v, e, order_v, mask_v, depth_v, wind_v, angle_v,
    col_v, water_v, wet_v, inv, nbr, nbr_mask, spd, fri, wx, wy, edge, coef, halo_out, halo_in, rim_out, rim_in, rim_sum, rim_all,
    part, part_in, total, total_in, damp_out, damp,
    ready, passed, in_sem, halo_send, halo_recv, rim_send, rim_recv, r_send, r_recv, a_send, a_recv, b_send, b_recv, c_send, c_recv,
):
    comps = e.shape[0]
    rows, lanes = order_v.shape
    tile = lax.axis_index("tile")
    comp = lax.axis_index("comp")
    q = lax.rem(comp, GROUP)
    y = lax.div(comp, GROUP)
    first = comp * comps
    f0 = lax.div(first, ND)
    f1 = lax.div(first + comps - 1, ND)
    has = (tile < tiles - 1, tile > 0)
    beside = (tile + 1, tile - 1)
    group = [(tile, y * GROUP + lax.rem(q + o, GROUP)) for o in range(GROUP)]
    ring = [(tile, lax.rem(y + o, y_count) * GROUP + q) for o in range(y_count)]
    order_a = sorted(range(1, GROUP), key=lambda o: abs(2 * o - GROUP))
    order_b = sorted(range(1, y_count), key=lambda o: abs(2 * o - y_count))
    inner = slice(8, rows + 8)

    copies = [
        pltpu.make_async_copy(src, dst, in_sem.at[i])
        for i, (src, dst) in enumerate(
            [(order_hbm, order_v), (mask_hbm, mask_v), (depth_hbm, depth_v),
             (wind_hbm, wind_v), (angle_hbm, angle_v), (speed_hbm, speed_s), (friction_hbm, friction_s),
             (const_hbm, const_s), (spectrum_hbm, e.at[:, inner, :]), (cos_hbm, cos_v)]
        )
    ]
    for copy in copies:
        copy.start()

    barrier = pltpu.get_barrier_semaphore()
    for to in [group[o] for o in order_a] + [ring[1], ring[y_count - 1]]:
        pl.semaphore_signal(barrier, inc=1, device_id=to, device_id_type=MESH)
    @pl.when(has[0])
    def _():
        for n in range(GROUP):
            pl.semaphore_signal(barrier, inc=1, device_id=(beside[0], y * GROUP + n), device_id_type=MESH)

    zero8 = jnp.zeros((8, lanes), jnp.float32)
    none8 = jnp.full((8, lanes), -1, jnp.int32)
    for pad in (slice(0, 8), slice(rows + 8, rows + 16)):
        for k in range(comps):
            e[k, pad, :] = zero8
        for h in range(2):
            inv[h, pad, :] = none8
            spd[h, pad, :] = zero8

    for copy in copies[:8]:
        copy.wait()
    copies[9].wait()
    sub = lax.broadcasted_iota(jnp.int32, (8, lanes), 0)
    spot = lax.broadcasted_iota(jnp.int32, (8, lanes), 1)
    groups = [slice(8 * n, 8 * n + 8) for n in range(GROUP)]
    inners = [slice(8 * n + 8, 8 * n + 16) for n in range(GROUP)]
    classes = [
        [(speed_s[n, f], friction_s[n, f]) for n in range(8)] for f in (f0, f1)
    ]
    for n, at in enumerate(groups):
        column = order_v[at, :] - (sub + 8 * n) * (2 * lanes)
        index = column & (lanes - 1)
        upper = column >= lanes
        cell = [
            jnp.where(upper, take(v[at, lanes:], index), take(v[at, :lanes], index))
            for v in (mask_v, depth_v, wind_v, angle_v)
        ]
        wet = cell[0] > 0
        water = jnp.where(wet, 1.0, 0.0)
        col_v[at, :] = column
        water_v[at, :] = water
        wet_v[at, :] = jnp.where(wet, column, 4 * lanes)
        wx[at, :] = cell[2]
        wy[at, :] = cell[3]
        s = [jnp.full((8, lanes), c[0][0]) for c in classes]
        r = [jnp.full((8, lanes), c[0][1]) for c in classes]
        for m in range(1, 8):
            here = cell[1] == m
            for i in range(2):
                s[i] = jnp.where(here, classes[i][m][0], s[i])
                r[i] = jnp.where(here, classes[i][m][1], r[i])
        for i in range(2):
            spd[i, inners[n], :] = s[i] * water
            fri[i, at, :] = r[i]

    narrow = jnp.int16
    lane = lax.broadcasted_iota(jnp.int32, (rows, lanes), 1)
    near = lane.astype(narrow)
    far = (lane + lanes).astype(narrow)
    here = wet_v[...].astype(narrow)
    low = jnp.full((rows, lanes), -1, narrow)
    high = low
    for j in range(lanes):
        turned = here if j == 0 else pltpu.roll(here, j, 1)
        slot = ((lane - j) & (lanes - 1)).astype(narrow)
        low = jnp.where(turned == near, slot, low)
        high = jnp.where(turned == far, slot, high)
    inv[0, inner, :] = low.astype(jnp.int32)
    inv[1, inner, :] = high.astype(jnp.int32)

    for n, at in enumerate(groups):
        column = col_v[at, :]
        water = water_v[at, :]
        index = column & (lanes - 1)
        upper = column >= lanes
        for b in range(2):
            rows_at = slice(8 * n + 7 + 2 * b, 8 * n + 15 + 2 * b)
            found = jnp.where(upper, take(inv[1, rows_at, :], index), take(inv[0, rows_at, :], index))
            nbr[b, at, :] = jnp.maximum(found, 0)
            nbr_mask[b, at, :] = jnp.where(found >= 0, water, 0.0)
        for b in range(2):
            shifted = column - 1 + 2 * b
            index = shifted & (lanes - 1)
            found = jnp.where(shifted >= lanes, take(inv[1, inners[n], :], index), take(inv[0, inners[n], :], index))
            inside = (shifted >= 0) & (shifted < 2 * lanes) & (found >= 0)
            nbr[2 + b, at, :] = jnp.maximum(found, 0)
            nbr_mask[2 + b, at, :] = jnp.where(inside, water, 0.0)

    copies[8].wait()
    pad = edge.shape[1]
    comp_at = first + lax.broadcasted_iota(jnp.int32, (pad, lanes), 0)
    second = comp_at >= ND * (f0 + 1)
    turn = (((comp_at & (ND - 1)) + 8) >> 4) & 1
    spread = jnp.abs(cos_v[pl.ds(lax.rem(first, ND), pad), :])
    for b in range(2):
        for i in range(2):
            coef[2 * b + i] = jnp.where((turn == b) & (second == (i == 1)), spread, 0.0)
    for b, at in ((0, rows - 1), (1, 0)):
        speed = jnp.where(second, spd[1, 8 + at : 9 + at, :], spd[0, 8 + at : 9 + at, :])
        edge[b, :comps, :] = e[:, 8 + at, :] * speed[:comps]

    w0 = const_s[2 * ND + NF + f0]
    w1 = const_s[2 * ND + NF + f1]
    v0 = w0 * const_s[2 * ND + f0]
    v1 = w1 * const_s[2 * ND + f1]
    for b, at in ((0, rows - 1), (1, 0)):
        back = [inv[h, 8 + at : 9 + at, :] for h in range(2)]
        for h in range(2):
            found = jnp.broadcast_to(back[h], (pad, lanes))
            halo_out[b, h] = jnp.where(found >= 0, take(edge[b], jnp.maximum(found, 0)), 0.0)
        s0 = jnp.sum((edge[b] * coef[2 * b])[:comps], axis=0, keepdims=True)
        s1 = jnp.sum((edge[b] * coef[2 * b + 1])[:comps], axis=0, keepdims=True)
        both = jnp.where(lax.rem(sub, 2) == 0, w0 * s0 + w1 * s1, v0 * s0 + v1 * s1)
        found = jnp.where(sub < 2, back[0], back[1])
        rim_out[b] = jnp.where(found >= 0, take(both, jnp.maximum(found, 0)), 0.0)

    def halo(b, to):
        return pltpu.make_async_remote_copy(
            src_ref=halo_out.at[b], dst_ref=halo_in.at[b], send_sem=halo_send.at[b], recv_sem=halo_recv.at[b],
            device_id=(to, comp), device_id_type=MESH,
        )

    def rim(b, n):
        return pltpu.make_async_remote_copy(
            src_ref=rim_out.at[b], dst_ref=rim_in.at[b, q], send_sem=rim_send.at[b], recv_sem=rim_recv.at[b],
            device_id=(beside[b], y * GROUP + n), device_id_type=MESH,
        )

    def drain(ref, sem):
        pltpu.make_async_copy(ref, ref, sem).wait()

    def send_beside(b):
        for n in (3, 4, 2, 5, 1, 6, 0, 7):
            rim(b, n).start()
        halo(b, beside[b]).start()

    def relay(step):
        for o in (step + 1, y_count - step - 1):
            pl.semaphore_signal(passed.at[step], inc=1, device_id=ring[o], device_id_type=MESH)

    def announce():
        pl.semaphore_wait(barrier, GROUP + 1 + GROUP * lax.div(tile + tiles - 1, tiles))

        relay(0)

        @pl.when(has[1])
        def _():
            for n in range(GROUP):
                pl.semaphore_signal(ready, inc=1, device_id=(beside[1], y * GROUP + n), device_id_type=MESH)
            send_beside(1)

    late = jnp.abs(2 * y - y_count) <= 2
    pl.when(late)(announce)

    def advect(step, carry):
        sums = list(carry)
        for pair in range(3):
            advect_pair(6 * step + 2 * pair, sums)
        return tuple(sums)

    def advect_pair(k, sums):
        f = lax.div(first + k, ND)
        d = lax.rem(first + k, ND)
        i = f - f0
        bx = lax.rem(lax.div(d + 8, 16), 2)
        by = lax.div(d, 16)
        weight = const_s[2 * ND + NF + f]
        weight_freq = weight * const_s[2 * ND + f]
        cos = [jnp.abs(const_s[d + u]) for u in range(2)]
        sin = [jnp.abs(const_s[ND + d + u]) for u in range(2)]
        for n, at in enumerate(groups):
            speed = spd[i, inners[n], :]
            behind = pl.ds(8 * n + 7 + 2 * bx, 8)
            speed_x = spd[i, behind, :]
            energy = [e[k + u, inners[n], :] for u in range(2)]
            flux = [energy[u] * speed for u in range(2)]
            flux_x = [e[k + u, behind, :] * speed_x for u in range(2)]
            index = nbr[bx, at, :]
            gx = [take(flux_x[u], index) for u in range(2)]
            index = nbr[2 + by, at, :]
            gy = [take(flux[u], index) for u in range(2)]
            mask_x = nbr_mask[bx, at, :]
            mask_y = nbr_mask[2 + by, at, :]
            water = water_v[at, :]
            for u in range(2):
                moved = energy[u] * water - (cos[u] + sin[u]) * flux[u]
                moved = moved + cos[u] * (mask_x * gx[u]) + sin[u] * (mask_y * gy[u])
                p_ref[k + u, at, :] = moved
                sums[n] = sums[n] + weight * moved
                sums[GROUP + n] = sums[GROUP + n] + weight_freq * moved

    zero = jnp.zeros((8, lanes), jnp.float32)
    sums = lax.fori_loop(0, comps // 6, advect, (zero,) * (2 * GROUP))
    for n in range(GROUP):
        part[n, 0] = sums[n]
        part[n, 1] = sums[GROUP + n]

    pl.when(jnp.logical_not(late))(announce)

    scatters = {
        o: pltpu.make_async_remote_copy(
            src_ref=part.at[lax.rem(q + o, GROUP)], dst_ref=part_in.at[o - 1], send_sem=a_send, recv_sem=a_recv,
            device_id=group[o], device_id_type=MESH,
        )
        for o in order_a
    }
    for o in order_a:
        scatters[o].start()

    pl.semaphore_wait(passed.at[0], 2)
    if y_count > 4:
        relay(1)

    wind = 0.05 * wx[...]
    angle = wy[...]
    wx[...] = wind * jnp.cos(angle)
    wy[...] = wind * jnp.sin(angle)

    drain(part_in, a_recv)
    for h in range(2):
        held = part[q, h]
        for n in range(GROUP - 1):
            held += part_in[n, h]
        total[h] = held

    if y_count > 4:
        pl.semaphore_wait(passed.at[1], 2)
    exchanges = {
        o: pltpu.make_async_remote_copy(
            src_ref=total, dst_ref=total_in.at[o - 1], send_sem=b_send, recv_sem=b_recv,
            device_id=ring[o], device_id_type=MESH,
        )
        for o in order_b
    }
    for o in order_b:
        exchanges[o].start()

    @pl.when(has[0])
    def _():
        pl.semaphore_wait(ready, GROUP)
        send_beside(0)

    for b, at in ((0, 0), (1, rows - 1)):
        @pl.when(has[1 - b])
        def _():
            halo(b, beside[1 - b]).wait_recv()
            column1 = jnp.broadcast_to(col_v[at : at + 1, :], (pad, lanes))
            came = take_wide(halo_in[b, 0], halo_in[b, 1], column1) * water_v[at : at + 1, :]
            came = came * (coef[2 * b] + coef[2 * b + 1])
            for k in range(comps):
                p_ref[k, at : at + 1, :] += came[k : k + 1]

    def sources(step, carry):
        for u in range(3):
            k = step * 3 + u
            f = lax.div(first + k, ND)
            d = lax.rem(first + k, ND)
            freq = const_s[2 * ND + f]
            push = jnp.maximum((freq * const_s[d]) * wx[...] + (freq * const_s[ND + d]) * wy[...] - 0.05, 0.0)
            p_ref[k] = p_ref[k] * jnp.exp(push - fri[f - f0])
        return carry

    lax.fori_loop(0, comps // 3, sources, 0)

    for b in range(2):
        rim_sum[b] = jnp.zeros((8, lanes), jnp.float32)

        @pl.when(has[1 - b])
        def _():
            drain(rim_in.at[b], rim_recv.at[b])
            came = rim_in[b, 0]
            for n in range(1, GROUP):
                came += rim_in[b, n]
            rim_sum[b] = came

    rims = {
        o: pltpu.make_async_remote_copy(
            src_ref=rim_sum, dst_ref=rim_all.at[o - 1], send_sem=r_send, recv_sem=r_recv,
            device_id=ring[o], device_id_type=MESH,
        )
        for o in order_b
    }
    for o in order_b:
        rims[o].start()

    drain(total_in, b_recv)
    a0 = total[0]
    a1 = total[1]
    for n in range(y_count - 1):
        a0 += total_in[n, 0]
        a1 += total_in[n, 1]

    def damping(m0, m1, wet):
        mean = jnp.where(wet, m1 / jnp.where(wet, m0, 1.0), 1.0)
        square = mean * mean
        alpha = m0 * (square * square)
        return 2.0 * alpha * alpha / mean

    outer = lax.div(q, GROUP - 1)
    rim0 = jnp.where(outer == 1, a0[7:8], a0[0:1])
    rim1 = jnp.where(outer == 1, a1[7:8], a1[0:1])
    wet_here = water_v[pl.ds(pl.multiple_of(q * 8, 8), 8), :] > 0
    mine = damping(a0, a1, wet_here)
    damp_out[0] = mine
    damp_out[1] = jnp.where(sub == 0, rim0, rim1)
    gathers = {
        o: pltpu.make_async_remote_copy(
            src_ref=damp_out, dst_ref=damp.at[q], send_sem=c_send, recv_sem=c_recv,
            device_id=group[o], device_id_type=MESH,
        )
        for o in order_a
    }
    for o in order_a:
        gathers[o].start()
    damp[q, 0] = mine
    damp[q, 1] = damp_out[1]
    drain(rim_all, r_recv)
    added = []
    for b, at in ((0, 0), (1, rows - 1)):
        came = rim_sum[b]
        for n in range(y_count - 1):
            came += rim_all[n, b]
        column1 = col_v[at : at + 1, :]
        found = take(came, jnp.broadcast_to(column1 & (lanes - 1), (8, lanes)))
        ours = water_v[at : at + 1, :]
        added.append(jnp.where(column1 >= lanes, found[2:4], found[0:2]) * ours)
    drain(damp.at[pl.ds(0, GROUP - 1)], c_recv)
    factor = [damp[n, 0] for n in range(GROUP)]
    for b, n, at in ((0, 0, 0), (1, GROUP - 1, rows - 1)):
        both = damp[n, 1][0:2] + added[b]
        fixed = damping(both[0:1], both[1:2], water_v[at : at + 1, :] > 0)
        factor[n] = jnp.where(sub == at % 8, fixed, factor[n])
    for n, at in enumerate(groups):
        wx[at, :] = jnp.exp(-const_s[2 * ND + f0] * factor[n])
        wy[at, :] = jnp.exp(-const_s[2 * ND + f1] * factor[n])
    for k in range(0, comps, 2):
        fade = jnp.where(lax.div(first + k, ND) == f0, wx[...], wy[...])
        for u in range(2):
            x_ref[k + u] = p_ref[k + u] * fade

    drain(part_in, a_send)
    drain(total_in, b_send)
    drain(rim_all, r_send)
    drain(damp.at[pl.ds(0, GROUP - 1)], c_send)
    for b in range(2):
        @pl.when(has[b])
        def _():
            drain(rim_in.at[b], rim_send.at[b])
            halo(b, beside[b]).wait_send()


def body(tiles, y_count, spectrum, sea_mask, sea_order, depth_class, wind_speed, wind_angle, speed_table, friction_table):
    comps = spectrum.shape[0]
    rows = sea_mask.shape[0]
    f32, i32 = jnp.float32, jnp.int32
    hbm = pl.BlockSpec(memory_space=pltpu.HBM)
    vmem = pl.BlockSpec(memory_space=pltpu.VMEM)
    grid = (rows, LANES)
    wide = (rows, 2 * LANES)
    pad = -(-comps // 8) * 8
    V, S, D = pltpu.VMEM, pltpu.SMEM, pltpu.SemaphoreType.DMA
    numbers = constants()
    table = jnp.asarray(numbers)
    doubled = jnp.asarray(np.ascontiguousarray(np.broadcast_to(np.tile(numbers[:ND], 2)[:, None], (2 * ND, LANES))))
    operands = (
        spectrum.reshape(comps, rows, LANES), sea_order.reshape(grid), sea_mask, depth_class, wind_speed, wind_angle,
        speed_table, friction_table, table, doubled,
    )
    result = pl.pallas_call(
        functools.partial(step_kernel, tiles, y_count),
        out_shape=jax.ShapeDtypeStruct((comps,) + grid, f32),
        in_specs=[hbm] * 10,
        out_specs=vmem,
        scratch_shapes=[
            V((comps,) + grid, f32),
            S(speed_table.shape, f32), S(friction_table.shape, f32), S(table.shape, f32),
            V(doubled.shape, f32), V((comps, rows + 16, LANES), f32),
            V(grid, i32), V(wide, i32), V(wide, i32), V(wide, f32), V(wide, f32),
            V(grid, i32), V(grid, f32), V(grid, i32), V((2, rows + 16, LANES), i32), V((4,) + grid, i32), V((4,) + grid, f32),
            V((2, rows + 16, LANES), f32), V((2,) + grid, f32),
            V(grid, f32), V(grid, f32), V((2, pad, LANES), f32), V((4, pad, LANES), f32),
            V((2, 2, pad, LANES), f32), V((2, 2, pad, LANES), f32), V((2, 8, LANES), f32), V((2, GROUP, 8, LANES), f32),
            V((2, 8, LANES), f32), V((y_count - 1, 2, 8, LANES), f32),
            V((GROUP, 2, 8, LANES), f32), V((GROUP - 1, 2, 8, LANES), f32),
            V((2, 8, LANES), f32), V((y_count - 1, 2, 8, LANES), f32),
            V((2, 8, LANES), f32), V((GROUP, 2, 8, LANES), f32),
            pltpu.SemaphoreType.REGULAR, pltpu.SemaphoreType.REGULAR((2,)), D((10,)), D((2,)), D((2,)), D((2,)), D((2,)), D, D, D, D, D, D, D, D,
        ],
        compiler_params=pltpu.CompilerParams(collective_id=0, has_side_effects=True, vmem_limit_bytes=32 << 20),
        name="wave_step",
    )(*[pltpu.with_memory_space_constraint(z, pltpu.HBM) for z in operands])
    return result.reshape(spectrum.shape)


def solution(mesh):
    return jax.shard_map(
        functools.partial(body, mesh.shape["tile"], mesh.shape["comp"] // GROUP),
        mesh=mesh,
        in_specs=(
            P("comp", "tile", None),
            P("tile", None),
            P("tile", None),
            P("tile", None),
            P("tile", None),
            P("tile", None),
            P(),
            P(),
        ),
        out_specs=P("comp", "tile", None),
        check_vma=False,
    )
```

```python
import functools
import math

import jax
import jax.numpy as jnp
import numpy as np
from jax import lax
from jax.experimental import pallas as pl
from jax.experimental.pallas import tpu as pltpu
from jax.sharding import PartitionSpec as P

NF = 36
ND = 32
LANES = 128
GROUP = 8
MESH = pl.DeviceIdType.MESH


def constants():
    theta = (np.arange(ND) + 0.5) * (2.0 * math.pi / ND)
    freq = 0.04 * np.exp(np.arange(NF) * (math.log(28.0) / (NF - 1)))
    weight = 0.1 * freq * (2.0 * math.pi / ND)
    return np.concatenate([np.cos(theta), np.sin(theta), freq, weight]).astype(np.float32)


def take(x, index):
    return lax.gather(
        x, index[..., None],
        lax.GatherDimensionNumbers((), (1,), (1,), (0,), (0,)),
        (1, 1), mode=lax.GatherScatterMode.PROMISE_IN_BOUNDS,
    )


def take_wide(low, high, column):
    index = column & (LANES - 1)
    return jnp.where(column >= LANES, take(high, index), take(low, index))


def step_kernel(
    tiles, y_count,
    spectrum_hbm, order_hbm, mask_hbm, depth_hbm, wind_hbm, angle_hbm, speed_hbm, friction_hbm, const_hbm, cos_hbm,
    x_ref, p_ref,
    speed_s, friction_s, const_s,
    cos_v, e, order_v, mask_v, depth_v, wind_v, angle_v,
    col_v, water_v, wet_v, inv, nbr, nbr_mask, spd, fri, wx, wy, edge, coef, halo_out, halo_in, rim_out, rim_in, rim_sum, rim_all,
    part, part_in, total, total_in, damp_out, damp,
    ready, passed, in_sem, halo_send, halo_recv, rim_send, rim_recv, r_send, r_recv, a_send, a_recv, b_send, b_recv, c_send, c_recv,
):
    comps = e.shape[0]
    rows, lanes = order_v.shape
    tile = lax.axis_index("tile")
    comp = lax.axis_index("comp")
    q = lax.rem(comp, GROUP)
    y = lax.div(comp, GROUP)
    first = comp * comps
    f0 = lax.div(first, ND)
    f1 = lax.div(first + comps - 1, ND)
    has = (tile < tiles - 1, tile > 0)
    beside = (tile + 1, tile - 1)
    group = [(tile, y * GROUP + lax.rem(q + o, GROUP)) for o in range(GROUP)]
    ring = [(tile, lax.rem(y + o, y_count) * GROUP + q) for o in range(y_count)]
    order_a = sorted(range(1, GROUP), key=lambda o: abs(2 * o - GROUP))
    order_b = sorted(range(1, y_count), key=lambda o: abs(2 * o - y_count))
    inner = slice(8, rows + 8)

    copies = [
        pltpu.make_async_copy(src, dst, in_sem.at[i])
        for i, (src, dst) in enumerate(
            [(order_hbm, order_v), (mask_hbm, mask_v), (depth_hbm, depth_v),
             (wind_hbm, wind_v), (angle_hbm, angle_v), (speed_hbm, speed_s), (friction_hbm, friction_s),
             (const_hbm, const_s), (spectrum_hbm, e.at[:, inner, :]), (cos_hbm, cos_v)]
        )
    ]
    for copy in copies:
        copy.start()

    barrier = pltpu.get_barrier_semaphore()
    for to in [group[o] for o in order_a] + [ring[1], ring[y_count - 1]]:
        pl.semaphore_signal(barrier, inc=1, device_id=to, device_id_type=MESH)
    @pl.when(has[0])
    def _():
        for n in range(GROUP):
            pl.semaphore_signal(barrier, inc=1, device_id=(beside[0], y * GROUP + n), device_id_type=MESH)

    zero8 = jnp.zeros((8, lanes), jnp.float32)
    for rim_rows in (slice(0, 8), slice(rows + 8, rows + 16)):
        inv[rim_rows, :] = jnp.zeros((8, lanes), jnp.int32)
        for k in range(comps):
            e[k, rim_rows, :] = zero8
        for h in range(2):
            spd[h, rim_rows, :] = zero8

    for copy in copies[:3] + copies[5:8]:
        copy.wait()
    sub = lax.broadcasted_iota(jnp.int32, (8, lanes), 0)
    spot = lax.broadcasted_iota(jnp.int32, (8, lanes), 1)
    groups = [slice(8 * n, 8 * n + 8) for n in range(GROUP)]
    inners = [slice(8 * n + 8, 8 * n + 16) for n in range(GROUP)]
    classes = [
        [(speed_s[n, f], friction_s[n, f]) for n in range(8)] for f in (f0, f1)
    ]
    for n, at in enumerate(groups):
        column = order_v[at, :] - (sub + 8 * n) * (2 * lanes)
        index = column & (lanes - 1)
        upper = column >= lanes
        halves = [mask_v[at, h] + 2 * depth_v[at, h] for h in (slice(0, lanes), slice(lanes, 2 * lanes))]
        cell = jnp.where(upper, take(halves[1], index), take(halves[0], index))
        wet = (cell & 1) > 0
        kind = cell >> 1
        water = jnp.where(wet, 1.0, 0.0)
        col_v[at, :] = column
        water_v[at, :] = water
        wet_v[at, :] = jnp.where(wet, column, 4 * lanes)
        s = [jnp.full((8, lanes), c[0][0]) for c in classes]
        r = [jnp.full((8, lanes), c[0][1]) for c in classes]
        for m in range(1, 8):
            here = kind == m
            for i in range(2):
                s[i] = jnp.where(here, classes[i][m][0], s[i])
                r[i] = jnp.where(here, classes[i][m][1], r[i])
        for i in range(2):
            spd[i, inners[n], :] = s[i] * water
            fri[i, at, :] = r[i]

    narrow = jnp.int16
    lane = lax.broadcasted_iota(jnp.int32, (rows, lanes), 1)
    near = lane.astype(narrow)
    far = (lane + lanes).astype(narrow)
    here = wet_v[...].astype(narrow)
    low = jnp.full((rows, lanes), -1, narrow)
    high = low
    for j in range(lanes):
        turned = here if j == 0 else pltpu.roll(here, j, 1)
        slot = ((lane - j) & (lanes - 1)).astype(narrow)
        low = jnp.where(turned == near, slot, low)
        high = jnp.where(turned == far, slot, high)
    inv[inner, :] = (low.astype(jnp.int32) + 1) | ((high.astype(jnp.int32) + 1) << 8)

    for n, at in enumerate(groups):
        column = col_v[at, :]
        water = water_v[at, :]
        index = column & (lanes - 1)
        upper = column >= lanes
        got = take(inv[8 * n + 7 : 8 * n + 15, :] | (inv[8 * n + 9 : 8 * n + 17, :] << 16), index)
        got = jnp.where(upper, got >> 8, got)
        for b in range(2):
            found = ((got >> 16 if b else got) & 255) - 1
            nbr[b, at, :] = jnp.maximum(found, 0)
            nbr_mask[b, at, :] = jnp.where(found >= 0, water, 0.0)
        for b in range(2):
            shifted = column - 1 + 2 * b
            got = take(inv[inners[n], :], shifted & (lanes - 1))
            found = (jnp.where(shifted >= lanes, got >> 8, got) & 255) - 1
            inside = (shifted >= 0) & (shifted < 2 * lanes) & (found >= 0)
            nbr[2 + b, at, :] = jnp.maximum(found, 0)
            nbr_mask[2 + b, at, :] = jnp.where(inside, water, 0.0)

    copies[8].wait()
    copies[9].wait()
    pad = edge.shape[1]
    comp_at = first + lax.broadcasted_iota(jnp.int32, (pad, lanes), 0)
    second = comp_at >= ND * (f0 + 1)
    turn = (((comp_at & (ND - 1)) + 8) >> 4) & 1
    spread = jnp.abs(cos_v[pl.ds(lax.rem(first, ND), pad), :])
    for b in range(2):
        for i in range(2):
            coef[2 * b + i] = jnp.where((turn == b) & (second == (i == 1)), spread, 0.0)
    for b, at in ((0, rows - 1), (1, 0)):
        speed = jnp.where(second, spd[1, 8 + at : 9 + at, :], spd[0, 8 + at : 9 + at, :])
        edge[b, :comps, :] = e[:, 8 + at, :] * speed[:comps]

    w0 = const_s[2 * ND + NF + f0]
    w1 = const_s[2 * ND + NF + f1]
    v0 = w0 * const_s[2 * ND + f0]
    v1 = w1 * const_s[2 * ND + f1]
    for b, at in ((0, rows - 1), (1, 0)):
        packed = inv[8 + at : 9 + at, :]
        back = [(packed & 255) - 1, (packed >> 8) - 1]
        for h in range(2):
            found = jnp.broadcast_to(back[h], (pad, lanes))
            halo_out[b, h] = jnp.where(found >= 0, take(edge[b], jnp.maximum(found, 0)), 0.0)
        s0 = jnp.sum((edge[b] * coef[2 * b])[:comps], axis=0, keepdims=True)
        s1 = jnp.sum((edge[b] * coef[2 * b + 1])[:comps], axis=0, keepdims=True)
        both = jnp.where(lax.rem(sub, 2) == 0, w0 * s0 + w1 * s1, v0 * s0 + v1 * s1)
        found = jnp.where(sub < 2, back[0], back[1])
        rim_out[b] = jnp.where(found >= 0, take(both, jnp.maximum(found, 0)), 0.0)

    def halo(b, to):
        return pltpu.make_async_remote_copy(
            src_ref=halo_out.at[b], dst_ref=halo_in.at[b], send_sem=halo_send.at[b], recv_sem=halo_recv.at[b],
            device_id=(to, comp), device_id_type=MESH,
        )

    def rim(b, n):
        return pltpu.make_async_remote_copy(
            src_ref=rim_out.at[b], dst_ref=rim_in.at[b, q], send_sem=rim_send.at[b], recv_sem=rim_recv.at[b],
            device_id=(beside[b], y * GROUP + n), device_id_type=MESH,
        )

    def drain(ref, sem):
        pltpu.make_async_copy(ref, ref, sem).wait()

    def send_beside(b):
        for n in (3, 4, 2, 5, 1, 6, 0, 7):
            rim(b, n).start()
        halo(b, beside[b]).start()

    def relay(step):
        for o in (step + 1, y_count - step - 1):
            pl.semaphore_signal(passed.at[step], inc=1, device_id=ring[o], device_id_type=MESH)

    def announce():
        pl.semaphore_wait(barrier, GROUP + 1 + GROUP * lax.div(tile + tiles - 1, tiles))

        relay(0)

        @pl.when(has[1])
        def _():
            for n in range(GROUP):
                pl.semaphore_signal(ready, inc=1, device_id=(beside[1], y * GROUP + n), device_id_type=MESH)
            send_beside(1)

    late = jnp.abs(2 * y - y_count) <= 2
    pl.when(late)(announce)

    def advect(step, carry):
        sums = list(carry)
        for pair in range(3):
            advect_pair(6 * step + 2 * pair, sums)
        return tuple(sums)

    def advect_pair(k, sums):
        f = lax.div(first + k, ND)
        d = lax.rem(first + k, ND)
        i = f - f0
        bx = lax.rem(lax.div(d + 8, 16), 2)
        by = lax.div(d, 16)
        weight = const_s[2 * ND + NF + f]
        weight_freq = weight * const_s[2 * ND + f]
        cos = [jnp.abs(const_s[d + u]) for u in range(2)]
        sin = [jnp.abs(const_s[ND + d + u]) for u in range(2)]
        for n, at in enumerate(groups):
            speed = spd[i, inners[n], :]
            behind = pl.ds(8 * n + 7 + 2 * bx, 8)
            speed_x = spd[i, behind, :]
            energy = [e[k + u, inners[n], :] for u in range(2)]
            flux = [energy[u] * speed for u in range(2)]
            flux_x = [e[k + u, behind, :] * speed_x for u in range(2)]
            index = nbr[bx, at, :]
            gx = [take(flux_x[u], index) for u in range(2)]
            index = nbr[2 + by, at, :]
            gy = [take(flux[u], index) for u in range(2)]
            mask_x = nbr_mask[bx, at, :]
            mask_y = nbr_mask[2 + by, at, :]
            water = water_v[at, :]
            for u in range(2):
                moved = energy[u] * water - (cos[u] + sin[u]) * flux[u]
                moved = moved + cos[u] * (mask_x * gx[u]) + sin[u] * (mask_y * gy[u])
                p_ref[k + u, at, :] = moved
                sums[n] = sums[n] + weight * moved
                sums[GROUP + n] = sums[GROUP + n] + weight_freq * moved

    zero = jnp.zeros((8, lanes), jnp.float32)
    sums = lax.fori_loop(0, comps // 6, advect, (zero,) * (2 * GROUP))
    for n in range(GROUP):
        part[n, 0] = sums[n]
        part[n, 1] = sums[GROUP + n]

    pl.when(jnp.logical_not(late))(announce)

    scatters = {
        o: pltpu.make_async_remote_copy(
            src_ref=part.at[lax.rem(q + o, GROUP)], dst_ref=part_in.at[o - 1], send_sem=a_send, recv_sem=a_recv,
            device_id=group[o], device_id_type=MESH,
        )
        for o in order_a
    }
    for o in order_a:
        scatters[o].start()

    pl.semaphore_wait(passed.at[0], 2)
    if y_count > 4:
        relay(1)

    copies[3].wait()
    copies[4].wait()
    for at in groups:
        column = col_v[at, :]
        index = column & (lanes - 1)
        upper = column >= lanes
        wind = 0.05 * jnp.where(upper, take(wind_v[at, lanes:], index), take(wind_v[at, :lanes], index))
        angle = jnp.where(upper, take(angle_v[at, lanes:], index), take(angle_v[at, :lanes], index))
        wx[at, :] = wind * jnp.cos(angle)
        wy[at, :] = wind * jnp.sin(angle)

    drain(part_in, a_recv)
    for h in range(2):
        held = part[q, h]
        for n in range(GROUP - 1):
            held += part_in[n, h]
        total[h] = held

    if y_count > 4:
        pl.semaphore_wait(passed.at[1], 2)
    exchanges = {
        o: pltpu.make_async_remote_copy(
            src_ref=total, dst_ref=total_in.at[o - 1], send_sem=b_send, recv_sem=b_recv,
            device_id=ring[o], device_id_type=MESH,
        )
        for o in order_b
    }
    for o in order_b:
        exchanges[o].start()

    @pl.when(has[0])
    def _():
        pl.semaphore_wait(ready, GROUP)
        send_beside(0)

    for b, at in ((0, 0), (1, rows - 1)):
        @pl.when(has[1 - b])
        def _():
            halo(b, beside[1 - b]).wait_recv()
            column1 = jnp.broadcast_to(col_v[at : at + 1, :], (pad, lanes))
            came = take_wide(halo_in[b, 0], halo_in[b, 1], column1) * water_v[at : at + 1, :]
            came = came * (coef[2 * b] + coef[2 * b + 1])
            for k in range(comps):
                p_ref[k, at : at + 1, :] += came[k : k + 1]

    def sources(step, carry):
        for u in range(3):
            k = step * 3 + u
            f = lax.div(first + k, ND)
            d = lax.rem(first + k, ND)
            freq = const_s[2 * ND + f]
            push = jnp.maximum((freq * const_s[d]) * wx[...] + (freq * const_s[ND + d]) * wy[...] - 0.05, 0.0)
            p_ref[k] = p_ref[k] * jnp.exp(push - fri[f - f0])
        return carry

    lax.fori_loop(0, comps // 3, sources, 0)

    for b in range(2):
        rim_sum[b] = jnp.zeros((8, lanes), jnp.float32)

        @pl.when(has[1 - b])
        def _():
            drain(rim_in.at[b], rim_recv.at[b])
            came = rim_in[b, 0]
            for n in range(1, GROUP):
                came += rim_in[b, n]
            rim_sum[b] = came

    rims = {
        o: pltpu.make_async_remote_copy(
            src_ref=rim_sum, dst_ref=rim_all.at[o - 1], send_sem=r_send, recv_sem=r_recv,
            device_id=ring[o], device_id_type=MESH,
        )
        for o in order_b
    }
    for o in order_b:
        rims[o].start()

    drain(total_in, b_recv)
    a0 = total[0]
    a1 = total[1]
    for n in range(y_count - 1):
        a0 += total_in[n, 0]
        a1 += total_in[n, 1]

    def damping(m0, m1, wet):
        mean = jnp.where(wet, m1 / jnp.where(wet, m0, 1.0), 1.0)
        square = mean * mean
        alpha = m0 * (square * square)
        return 2.0 * alpha * alpha / mean

    outer = lax.div(q, GROUP - 1)
    rim0 = jnp.where(outer == 1, a0[7:8], a0[0:1])
    rim1 = jnp.where(outer == 1, a1[7:8], a1[0:1])
    wet_here = water_v[pl.ds(pl.multiple_of(q * 8, 8), 8), :] > 0
    mine = damping(a0, a1, wet_here)
    damp_out[0] = mine
    damp_out[1] = jnp.where(sub == 0, rim0, rim1)
    gathers = {
        o: pltpu.make_async_remote_copy(
            src_ref=damp_out, dst_ref=damp.at[q], send_sem=c_send, recv_sem=c_recv,
            device_id=group[o], device_id_type=MESH,
        )
        for o in order_a
    }
    for o in order_a:
        gathers[o].start()
    damp[q, 0] = mine
    damp[q, 1] = damp_out[1]
    drain(rim_all, r_recv)
    added = []
    for b, at in ((0, 0), (1, rows - 1)):
        came = rim_sum[b]
        for n in range(y_count - 1):
            came += rim_all[n, b]
        column1 = col_v[at : at + 1, :]
        found = take(came, jnp.broadcast_to(column1 & (lanes - 1), (8, lanes)))
        ours = water_v[at : at + 1, :]
        added.append(jnp.where(column1 >= lanes, found[2:4], found[0:2]) * ours)
    drain(damp.at[pl.ds(0, GROUP - 1)], c_recv)
    factor = [damp[n, 0] for n in range(GROUP)]
    for b, n, at in ((0, 0, 0), (1, GROUP - 1, rows - 1)):
        both = damp[n, 1][0:2] + added[b]
        fixed = damping(both[0:1], both[1:2], water_v[at : at + 1, :] > 0)
        factor[n] = jnp.where(sub == at % 8, fixed, factor[n])
    for n, at in enumerate(groups):
        wx[at, :] = jnp.exp(-const_s[2 * ND + f0] * factor[n])
        wy[at, :] = jnp.exp(-const_s[2 * ND + f1] * factor[n])
    for k in range(0, comps, 2):
        fade = jnp.where(lax.div(first + k, ND) == f0, wx[...], wy[...])
        for u in range(2):
            x_ref[k + u] = p_ref[k + u] * fade

    drain(part_in, a_send)
    drain(total_in, b_send)
    drain(rim_all, r_send)
    drain(damp.at[pl.ds(0, GROUP - 1)], c_send)
    for b in range(2):
        @pl.when(has[b])
        def _():
            drain(rim_in.at[b], rim_send.at[b])
            halo(b, beside[b]).wait_send()


def body(tiles, y_count, spectrum, sea_mask, sea_order, depth_class, wind_speed, wind_angle, speed_table, friction_table):
    comps = spectrum.shape[0]
    rows = sea_mask.shape[0]
    f32, i32 = jnp.float32, jnp.int32
    hbm = pl.BlockSpec(memory_space=pltpu.HBM)
    vmem = pl.BlockSpec(memory_space=pltpu.VMEM)
    grid = (rows, LANES)
    wide = (rows, 2 * LANES)
    pad = -(-comps // 8) * 8
    V, S, D = pltpu.VMEM, pltpu.SMEM, pltpu.SemaphoreType.DMA
    numbers = constants()
    table = jnp.asarray(numbers)
    doubled = jnp.asarray(np.ascontiguousarray(np.broadcast_to(np.tile(numbers[:ND], 2)[:, None], (2 * ND, LANES))))
    operands = (
        spectrum.reshape(comps, rows, LANES), sea_order.reshape(grid), sea_mask, depth_class, wind_speed, wind_angle,
        speed_table, friction_table, table, doubled,
    )
    result = pl.pallas_call(
        functools.partial(step_kernel, tiles, y_count),
        out_shape=jax.ShapeDtypeStruct((comps,) + grid, f32),
        in_specs=[hbm] * 10,
        out_specs=vmem,
        scratch_shapes=[
            V((comps,) + grid, f32),
            S(speed_table.shape, f32), S(friction_table.shape, f32), S(table.shape, f32),
            V(doubled.shape, f32), V((comps, rows + 16, LANES), f32),
            V(grid, i32), V(wide, i32), V(wide, i32), V(wide, f32), V(wide, f32),
            V(grid, i32), V(grid, f32), V(grid, i32), V((rows + 16, LANES), i32), V((4,) + grid, i32), V((4,) + grid, f32),
            V((2, rows + 16, LANES), f32), V((2,) + grid, f32),
            V(grid, f32), V(grid, f32), V((2, pad, LANES), f32), V((4, pad, LANES), f32),
            V((2, 2, pad, LANES), f32), V((2, 2, pad, LANES), f32), V((2, 8, LANES), f32), V((2, GROUP, 8, LANES), f32),
            V((2, 8, LANES), f32), V((y_count - 1, 2, 8, LANES), f32),
            V((GROUP, 2, 8, LANES), f32), V((GROUP - 1, 2, 8, LANES), f32),
            V((2, 8, LANES), f32), V((y_count - 1, 2, 8, LANES), f32),
            V((2, 8, LANES), f32), V((GROUP, 2, 8, LANES), f32),
            pltpu.SemaphoreType.REGULAR, pltpu.SemaphoreType.REGULAR((2,)), D((10,)), D((2,)), D((2,)), D((2,)), D((2,)), D, D, D, D, D, D, D, D,
        ],
        compiler_params=pltpu.CompilerParams(collective_id=0, has_side_effects=True, vmem_limit_bytes=32 << 20),
        name="wave_step",
    )(*[pltpu.with_memory_space_constraint(z, pltpu.HBM) for z in operands])
    return result.reshape(spectrum.shape)


def solution(mesh):
    return jax.shard_map(
        functools.partial(body, mesh.shape["tile"], mesh.shape["comp"] // GROUP),
        mesh=mesh,
        in_specs=(
            P("comp", "tile", None),
            P("tile", None),
            P("tile", None),
            P("tile", None),
            P("tile", None),
            P("tile", None),
            P(),
            P(),
        ),
        out_specs=P("comp", "tile", None),
        check_vma=False,
    )
```

```python
import functools
import math

import jax
import jax.numpy as jnp
import numpy as np
from jax import lax
from jax.experimental import pallas as pl
from jax.experimental.pallas import tpu as pltpu
from jax.sharding import PartitionSpec as P

NF = 36
ND = 32
LANES = 128
GROUP = 8
MESH = pl.DeviceIdType.MESH


def constants():
    theta = (np.arange(ND) + 0.5) * (2.0 * math.pi / ND)
    freq = 0.04 * np.exp(np.arange(NF) * (math.log(28.0) / (NF - 1)))
    weight = 0.1 * freq * (2.0 * math.pi / ND)
    return np.concatenate([np.cos(theta), np.sin(theta), freq, weight]).astype(np.float32)


def take(x, index):
    return lax.gather(
        x, index[..., None],
        lax.GatherDimensionNumbers((), (1,), (1,), (0,), (0,)),
        (1, 1), mode=lax.GatherScatterMode.PROMISE_IN_BOUNDS,
    )


def take_wide(low, high, column):
    index = column & (LANES - 1)
    return jnp.where(column >= LANES, take(high, index), take(low, index))


def step_kernel(
    tiles, y_count,
    spectrum_hbm, order_hbm, mask_hbm, depth_hbm, wind_hbm, angle_hbm, speed_hbm, friction_hbm, const_hbm, cos_hbm,
    x_ref, p_ref,
    speed_s, friction_s, const_s,
    cos_v, e, order_v, mask_v, depth_v, wind_v, angle_v,
    col_v, water_v, wet_v, inv, nbr, nbr_mask, spd, fri, wx, wy, edge, coef, halo_out, halo_in, rim_out, rim_in, rim_sum, rim_all,
    gain, sent, part, part_in, total, total_in, damp_out, damp,
    ready, passed, in_sem, halo_send, halo_recv, rim_send, rim_recv, r_send, r_recv, a_send, a_recv, b_send, b_recv, c_send, c_recv,
):
    comps = e.shape[0]
    rows, lanes = order_v.shape
    tile = lax.axis_index("tile")
    comp = lax.axis_index("comp")
    q = lax.rem(comp, GROUP)
    y = lax.div(comp, GROUP)
    first = comp * comps
    f0 = lax.div(first, ND)
    f1 = lax.div(first + comps - 1, ND)
    has = (tile < tiles - 1, tile > 0)
    beside = (tile + 1, tile - 1)
    group = [(tile, y * GROUP + lax.rem(q + o, GROUP)) for o in range(GROUP)]
    ring = [(tile, lax.rem(y + o, y_count) * GROUP + q) for o in range(y_count)]
    order_a = sorted(range(1, GROUP), key=lambda o: abs(2 * o - GROUP))
    order_b = sorted(range(1, y_count), key=lambda o: abs(2 * o - y_count))
    inner = slice(8, rows + 8)

    copies = [
        pltpu.make_async_copy(src, dst, in_sem.at[i])
        for i, (src, dst) in enumerate(
            [(order_hbm, order_v), (mask_hbm, mask_v), (depth_hbm, depth_v),
             (wind_hbm, wind_v), (angle_hbm, angle_v), (speed_hbm, speed_s), (friction_hbm, friction_s),
             (const_hbm, const_s), (spectrum_hbm, e.at[:, inner, :]), (cos_hbm, cos_v)]
        )
    ]
    for copy in copies:
        copy.start()

    barrier = pltpu.get_barrier_semaphore()
    for to in [group[o] for o in order_a] + [ring[1], ring[y_count - 1]]:
        pl.semaphore_signal(barrier, inc=1, device_id=to, device_id_type=MESH)
    @pl.when(has[0])
    def _():
        for n in range(GROUP):
            pl.semaphore_signal(barrier, inc=1, device_id=(beside[0], y * GROUP + n), device_id_type=MESH)

    zero8 = jnp.zeros((8, lanes), jnp.float32)
    for rim_rows in (slice(0, 8), slice(rows + 8, rows + 16)):
        inv[rim_rows, :] = jnp.zeros((8, lanes), jnp.int32)
        for k in range(comps):
            e[k, rim_rows, :] = zero8
        for h in range(2):
            spd[h, rim_rows, :] = zero8

    for copy in copies[:3] + copies[5:8]:
        copy.wait()
    sub = lax.broadcasted_iota(jnp.int32, (8, lanes), 0)
    spot = lax.broadcasted_iota(jnp.int32, (8, lanes), 1)
    groups = [slice(8 * n, 8 * n + 8) for n in range(GROUP)]
    inners = [slice(8 * n + 8, 8 * n + 16) for n in range(GROUP)]
    classes = [
        [(speed_s[n, f], friction_s[n, f]) for n in range(8)] for f in (f0, f1)
    ]
    for n, at in enumerate(groups):
        column = order_v[at, :] - (sub + 8 * n) * (2 * lanes)
        index = column & (lanes - 1)
        upper = column >= lanes
        halves = [mask_v[at, h] + 2 * depth_v[at, h] for h in (slice(0, lanes), slice(lanes, 2 * lanes))]
        cell = jnp.where(upper, take(halves[1], index), take(halves[0], index))
        wet = (cell & 1) > 0
        kind = cell >> 1
        water = jnp.where(wet, 1.0, 0.0)
        col_v[at, :] = column
        water_v[at, :] = water
        wet_v[at, :] = jnp.where(wet, column, 4 * lanes)
        s = [jnp.full((8, lanes), c[0][0]) for c in classes]
        r = [jnp.full((8, lanes), c[0][1]) for c in classes]
        for m in range(1, 8):
            here = kind == m
            for i in range(2):
                s[i] = jnp.where(here, classes[i][m][0], s[i])
                r[i] = jnp.where(here, classes[i][m][1], r[i])
        for i in range(2):
            spd[i, inners[n], :] = s[i] * water
            fri[i, at, :] = r[i]

    copies[8].wait()
    gain[...] = jnp.zeros_like(gain)
    for a in range(8):
        for rim_rows in (slice(0, 8), slice(rows + 8, rows + 16)):
            sent[a, rim_rows, :] = zero8

    def gather_up(step, carry):
        for pair in range(3):
            k = 6 * step + 2 * pair
            d = lax.rem(first + k, ND)
            i = lax.div(first + k, ND) - f0
            bx = lax.rem(lax.div(d + 8, 16), 2)
            by = lax.div(d, 16)
            cos = [jnp.abs(const_s[d + u]) for u in range(2)]
            sin = [jnp.abs(const_s[ND + d + u]) for u in range(2)]
            energy = [e[k + u, inner, :] for u in range(2)]
            gain[i] += energy[0] + energy[1]
            gain[2 + 2 * bx + i] += cos[0] * energy[0] + cos[1] * energy[1]
            gain[6 + 2 * by + i] += sin[0] * energy[0] + sin[1] * energy[1]
        return carry

    lax.fori_loop(0, comps // 6, gather_up, 0)

    narrow = jnp.int16
    lane = lax.broadcasted_iota(jnp.int32, (rows, lanes), 1)
    near = lane.astype(narrow)
    far = (lane + lanes).astype(narrow)
    here = wet_v[...].astype(narrow)
    low = jnp.full((rows, lanes), -1, narrow)
    high = low
    for j in range(lanes):
        turned = here if j == 0 else pltpu.roll(here, j, 1)
        slot = ((lane - j) & (lanes - 1)).astype(narrow)
        low = jnp.where(turned == near, slot, low)
        high = jnp.where(turned == far, slot, high)
    inv[inner, :] = (low.astype(jnp.int32) + 1) | ((high.astype(jnp.int32) + 1) << 8)

    for n, at in enumerate(groups):
        column = col_v[at, :]
        water = water_v[at, :]
        index = column & (lanes - 1)
        upper = column >= lanes
        got = take(inv[8 * n + 7 : 8 * n + 15, :] | (inv[8 * n + 9 : 8 * n + 17, :] << 16), index)
        got = jnp.where(upper, got >> 8, got)
        for b in range(2):
            found = ((got >> 16 if b else got) & 255) - 1
            nbr[b, at, :] = jnp.maximum(found, 0)
            nbr_mask[b, at, :] = jnp.where(found >= 0, water, 0.0)
        for b in range(2):
            shifted = column - 1 + 2 * b
            got = take(inv[inners[n], :], shifted & (lanes - 1))
            found = (jnp.where(shifted >= lanes, got >> 8, got) & 255) - 1
            inside = (shifted >= 0) & (shifted < 2 * lanes) & (found >= 0)
            nbr[2 + b, at, :] = jnp.maximum(found, 0)
            nbr_mask[2 + b, at, :] = jnp.where(inside, water, 0.0)

    w0 = const_s[2 * ND + NF + f0]
    w1 = const_s[2 * ND + NF + f1]
    v0 = w0 * const_s[2 * ND + f0]
    v1 = w1 * const_s[2 * ND + f1]
    for n, at in enumerate(groups):
        speed = [spd[i, inners[n], :] for i in range(2)]
        scale = ((w0 * speed[0], w1 * speed[1]), (v0 * speed[0], v1 * speed[1]))
        water = water_v[at, :]
        plain = [gain[i, at, :] for i in range(2)]
        across = [[gain[2 + 2 * a + i, at, :] for i in range(2)] for a in range(4)]
        for h in range(2):
            side = [scale[h][0] * across[a][0] + scale[h][1] * across[a][1] for a in range(4)]
            weights = ((w0, w1), (v0, v1))[h]
            part[n, h] = water * (weights[0] * plain[0] + weights[1] * plain[1]) - (side[0] + side[1] + side[2] + side[3])
            for a in range(4):
                sent[2 * a + h, inners[n], :] = side[a]
    for n, at in enumerate(groups):
        for a in range(4):
            rows_at = slice(8 * n + 7 + 2 * a, 8 * n + 15 + 2 * a) if a < 2 else inners[n]
            index = nbr[a, at, :]
            mask = nbr_mask[a, at, :]
            for h in range(2):
                part[n, h] += mask * take(sent[2 * a + h, rows_at, :], index)
    for b, at in ((0, rows - 1), (1, 0)):
        packed = inv[8 + at : 9 + at, :]
        back = [(packed & 255) - 1, (packed >> 8) - 1]
        both = jnp.where(lax.rem(sub, 2) == 0, sent[2 * b, 8 + at : 9 + at, :], sent[2 * b + 1, 8 + at : 9 + at, :])
        found = jnp.where(sub < 2, back[0], back[1])
        rim_out[b] = jnp.where(found >= 0, take(both, jnp.maximum(found, 0)), 0.0)

    def halo(b, to):
        return pltpu.make_async_remote_copy(
            src_ref=halo_out.at[b], dst_ref=halo_in.at[b], send_sem=halo_send.at[b], recv_sem=halo_recv.at[b],
            device_id=(to, comp), device_id_type=MESH,
        )

    def rim(b, n):
        return pltpu.make_async_remote_copy(
            src_ref=rim_out.at[b], dst_ref=rim_in.at[b, q], send_sem=rim_send.at[b], recv_sem=rim_recv.at[b],
            device_id=(beside[b], y * GROUP + n), device_id_type=MESH,
        )

    def drain(ref, sem):
        pltpu.make_async_copy(ref, ref, sem).wait()

    def send_beside(b):
        for n in (3, 4, 2, 5, 1, 6, 0, 7):
            rim(b, n).start()

    def relay(step):
        for o in (step + 1, y_count - step - 1):
            pl.semaphore_signal(passed.at[step], inc=1, device_id=ring[o], device_id_type=MESH)

    def announce():
        pl.semaphore_wait(barrier, GROUP + 1 + GROUP * lax.div(tile + tiles - 1, tiles))

        relay(0)

        @pl.when(has[1])
        def _():
            for n in range(GROUP):
                pl.semaphore_signal(ready, inc=1, device_id=(beside[1], y * GROUP + n), device_id_type=MESH)
            send_beside(1)

    announce()

    scatters = {
        o: pltpu.make_async_remote_copy(
            src_ref=part.at[lax.rem(q + o, GROUP)], dst_ref=part_in.at[o - 1], send_sem=a_send, recv_sem=a_recv,
            device_id=group[o], device_id_type=MESH,
        )
        for o in order_a
    }
    for o in order_a:
        scatters[o].start()

    pl.semaphore_wait(passed.at[0], 2)
    if y_count > 4:
        relay(1)

    copies[9].wait()
    pad = edge.shape[1]
    comp_at = first + lax.broadcasted_iota(jnp.int32, (pad, lanes), 0)
    second = comp_at >= ND * (f0 + 1)
    turn = (((comp_at & (ND - 1)) + 8) >> 4) & 1
    spread = jnp.abs(cos_v[pl.ds(lax.rem(first, ND), pad), :])
    for b in range(2):
        for i in range(2):
            coef[2 * b + i] = jnp.where((turn == b) & (second == (i == 1)), spread, 0.0)
    for b, at in ((0, rows - 1), (1, 0)):
        speed = jnp.where(second, spd[1, 8 + at : 9 + at, :], spd[0, 8 + at : 9 + at, :])
        edge[b, :comps, :] = e[:, 8 + at, :] * speed[:comps]

    for b, at in ((0, rows - 1), (1, 0)):
        packed = inv[8 + at : 9 + at, :]
        for h in range(2):
            found = jnp.broadcast_to((packed >> 8 if h else packed & 255) - 1, (pad, lanes))
            halo_out[b, h] = jnp.where(found >= 0, take(edge[b], jnp.maximum(found, 0)), 0.0)

    @pl.when(has[1])
    def _():
        halo(1, beside[1]).start()

    def advect(step, carry):
        for pair in range(3):
            advect_pair(6 * step + 2 * pair)
        return carry

    def advect_pair(k):
        f = lax.div(first + k, ND)
        d = lax.rem(first + k, ND)
        i = f - f0
        bx = lax.rem(lax.div(d + 8, 16), 2)
        by = lax.div(d, 16)
        cos = [jnp.abs(const_s[d + u]) for u in range(2)]
        sin = [jnp.abs(const_s[ND + d + u]) for u in range(2)]
        for n, at in enumerate(groups):
            speed = spd[i, inners[n], :]
            behind = pl.ds(8 * n + 7 + 2 * bx, 8)
            speed_x = spd[i, behind, :]
            energy = [e[k + u, inners[n], :] for u in range(2)]
            flux = [energy[u] * speed for u in range(2)]
            flux_x = [e[k + u, behind, :] * speed_x for u in range(2)]
            index = nbr[bx, at, :]
            gx = [take(flux_x[u], index) for u in range(2)]
            index = nbr[2 + by, at, :]
            gy = [take(flux[u], index) for u in range(2)]
            mask_x = nbr_mask[bx, at, :]
            mask_y = nbr_mask[2 + by, at, :]
            water = water_v[at, :]
            for u in range(2):
                moved = energy[u] * water - (cos[u] + sin[u]) * flux[u]
                moved = moved + cos[u] * (mask_x * gx[u]) + sin[u] * (mask_y * gy[u])
                p_ref[k + u, at, :] = moved

    lax.fori_loop(0, comps // 6, advect, 0)

    copies[3].wait()
    copies[4].wait()
    for at in groups:
        column = col_v[at, :]
        index = column & (lanes - 1)
        upper = column >= lanes
        wind = 0.05 * jnp.where(upper, take(wind_v[at, lanes:], index), take(wind_v[at, :lanes], index))
        angle = jnp.where(upper, take(angle_v[at, lanes:], index), take(angle_v[at, :lanes], index))
        wx[at, :] = wind * jnp.cos(angle)
        wy[at, :] = wind * jnp.sin(angle)

    drain(part_in, a_recv)
    for h in range(2):
        held = part[q, h]
        for n in range(GROUP - 1):
            held += part_in[n, h]
        total[h] = held

    if y_count > 4:
        pl.semaphore_wait(passed.at[1], 2)
    exchanges = {
        o: pltpu.make_async_remote_copy(
            src_ref=total, dst_ref=total_in.at[o - 1], send_sem=b_send, recv_sem=b_recv,
            device_id=ring[o], device_id_type=MESH,
        )
        for o in order_b
    }
    for o in order_b:
        exchanges[o].start()

    @pl.when(has[0])
    def _():
        pl.semaphore_wait(ready, GROUP)
        send_beside(0)
        halo(0, beside[0]).start()

    for b, at in ((0, 0), (1, rows - 1)):
        @pl.when(has[1 - b])
        def _():
            halo(b, beside[1 - b]).wait_recv()
            column1 = jnp.broadcast_to(col_v[at : at + 1, :], (pad, lanes))
            came = take_wide(halo_in[b, 0], halo_in[b, 1], column1) * water_v[at : at + 1, :]
            came = came * (coef[2 * b] + coef[2 * b + 1])
            for k in range(comps):
                p_ref[k, at : at + 1, :] += came[k : k + 1]

    def sources(step, carry):
        for u in range(3):
            k = step * 3 + u
            f = lax.div(first + k, ND)
            d = lax.rem(first + k, ND)
            freq = const_s[2 * ND + f]
            push = jnp.maximum((freq * const_s[d]) * wx[...] + (freq * const_s[ND + d]) * wy[...] - 0.05, 0.0)
            p_ref[k] = p_ref[k] * jnp.exp(push - fri[f - f0])
        return carry

    lax.fori_loop(0, comps // 3, sources, 0)

    for b in range(2):
        rim_sum[b] = jnp.zeros((8, lanes), jnp.float32)

        @pl.when(has[1 - b])
        def _():
            drain(rim_in.at[b], rim_recv.at[b])
            came = rim_in[b, 0]
            for n in range(1, GROUP):
                came += rim_in[b, n]
            rim_sum[b] = came

    rims = {
        o: pltpu.make_async_remote_copy(
            src_ref=rim_sum, dst_ref=rim_all.at[o - 1], send_sem=r_send, recv_sem=r_recv,
            device_id=ring[o], device_id_type=MESH,
        )
        for o in order_b
    }
    for o in order_b:
        rims[o].start()

    drain(total_in, b_recv)
    a0 = total[0]
    a1 = total[1]
    for n in range(y_count - 1):
        a0 += total_in[n, 0]
        a1 += total_in[n, 1]

    def damping(m0, m1, wet):
        mean = jnp.where(wet, m1 / jnp.where(wet, m0, 1.0), 1.0)
        square = mean * mean
        alpha = m0 * (square * square)
        return 2.0 * alpha * alpha / mean

    outer = lax.div(q, GROUP - 1)
    rim0 = jnp.where(outer == 1, a0[7:8], a0[0:1])
    rim1 = jnp.where(outer == 1, a1[7:8], a1[0:1])
    wet_here = water_v[pl.ds(pl.multiple_of(q * 8, 8), 8), :] > 0
    mine = damping(a0, a1, wet_here)
    damp_out[0] = mine
    damp_out[1] = jnp.where(sub == 0, rim0, rim1)
    gathers = {
        o: pltpu.make_async_remote_copy(
            src_ref=damp_out, dst_ref=damp.at[q], send_sem=c_send, recv_sem=c_recv,
            device_id=group[o], device_id_type=MESH,
        )
        for o in order_a
    }
    for o in order_a:
        gathers[o].start()
    damp[q, 0] = mine
    damp[q, 1] = damp_out[1]
    drain(rim_all, r_recv)
    added = []
    for b, at in ((0, 0), (1, rows - 1)):
        came = rim_sum[b]
        for n in range(y_count - 1):
            came += rim_all[n, b]
        column1 = col_v[at : at + 1, :]
        found = take(came, jnp.broadcast_to(column1 & (lanes - 1), (8, lanes)))
        ours = water_v[at : at + 1, :]
        added.append(jnp.where(column1 >= lanes, found[2:4], found[0:2]) * ours)
    drain(damp.at[pl.ds(0, GROUP - 1)], c_recv)
    factor = [damp[n, 0] for n in range(GROUP)]
    for b, n, at in ((0, 0, 0), (1, GROUP - 1, rows - 1)):
        both = damp[n, 1][0:2] + added[b]
        fixed = damping(both[0:1], both[1:2], water_v[at : at + 1, :] > 0)
        factor[n] = jnp.where(sub == at % 8, fixed, factor[n])
    for n, at in enumerate(groups):
        wx[at, :] = jnp.exp(-const_s[2 * ND + f0] * factor[n])
        wy[at, :] = jnp.exp(-const_s[2 * ND + f1] * factor[n])
    for k in range(0, comps, 2):
        fade = jnp.where(lax.div(first + k, ND) == f0, wx[...], wy[...])
        for u in range(2):
            x_ref[k + u] = p_ref[k + u] * fade

    drain(part_in, a_send)
    drain(total_in, b_send)
    drain(rim_all, r_send)
    drain(damp.at[pl.ds(0, GROUP - 1)], c_send)
    for b in range(2):
        @pl.when(has[b])
        def _():
            drain(rim_in.at[b], rim_send.at[b])
            halo(b, beside[b]).wait_send()


def body(tiles, y_count, spectrum, sea_mask, sea_order, depth_class, wind_speed, wind_angle, speed_table, friction_table):
    comps = spectrum.shape[0]
    rows = sea_mask.shape[0]
    f32, i32 = jnp.float32, jnp.int32
    hbm = pl.BlockSpec(memory_space=pltpu.HBM)
    vmem = pl.BlockSpec(memory_space=pltpu.VMEM)
    grid = (rows, LANES)
    wide = (rows, 2 * LANES)
    pad = -(-comps // 8) * 8
    V, S, D = pltpu.VMEM, pltpu.SMEM, pltpu.SemaphoreType.DMA
    numbers = constants()
    table = jnp.asarray(numbers)
    doubled = jnp.asarray(np.ascontiguousarray(np.broadcast_to(np.tile(numbers[:ND], 2)[:, None], (2 * ND, LANES))))
    operands = (
        spectrum.reshape(comps, rows, LANES), sea_order.reshape(grid), sea_mask, depth_class, wind_speed, wind_angle,
        speed_table, friction_table, table, doubled,
    )
    result = pl.pallas_call(
        functools.partial(step_kernel, tiles, y_count),
        out_shape=jax.ShapeDtypeStruct((comps,) + grid, f32),
        in_specs=[hbm] * 10,
        out_specs=vmem,
        scratch_shapes=[
            V((comps,) + grid, f32),
            S(speed_table.shape, f32), S(friction_table.shape, f32), S(table.shape, f32),
            V(doubled.shape, f32), V((comps, rows + 16, LANES), f32),
            V(grid, i32), V(wide, i32), V(wide, i32), V(wide, f32), V(wide, f32),
            V(grid, i32), V(grid, f32), V(grid, i32), V((rows + 16, LANES), i32), V((4,) + grid, i32), V((4,) + grid, f32),
            V((2, rows + 16, LANES), f32), V((2,) + grid, f32),
            V(grid, f32), V(grid, f32), V((2, pad, LANES), f32), V((4, pad, LANES), f32),
            V((2, 2, pad, LANES), f32), V((2, 2, pad, LANES), f32), V((2, 8, LANES), f32), V((2, GROUP, 8, LANES), f32),
            V((2, 8, LANES), f32), V((y_count - 1, 2, 8, LANES), f32),
            V((10,) + grid, f32), V((8, rows + 16, LANES), f32),
            V((GROUP, 2, 8, LANES), f32), V((GROUP - 1, 2, 8, LANES), f32),
            V((2, 8, LANES), f32), V((y_count - 1, 2, 8, LANES), f32),
            V((2, 8, LANES), f32), V((GROUP, 2, 8, LANES), f32),
            pltpu.SemaphoreType.REGULAR, pltpu.SemaphoreType.REGULAR((2,)), D((10,)), D((2,)), D((2,)), D((2,)), D((2,)), D, D, D, D, D, D, D, D,
        ],
        compiler_params=pltpu.CompilerParams(collective_id=0, has_side_effects=True, vmem_limit_bytes=32 << 20),
        name="wave_step",
    )(*[pltpu.with_memory_space_constraint(z, pltpu.HBM) for z in operands])
    return result.reshape(spectrum.shape)


def solution(mesh):
    return jax.shard_map(
        functools.partial(body, mesh.shape["tile"], mesh.shape["comp"] // GROUP),
        mesh=mesh,
        in_specs=(
            P("comp", "tile", None),
            P("tile", None),
            P("tile", None),
            P("tile", None),
            P("tile", None),
            P("tile", None),
            P(),
            P(),
        ),
        out_specs=P("comp", "tile", None),
        check_vma=False,
    )
```

```python
import functools
import math

import jax
import jax.numpy as jnp
import numpy as np
from jax import lax
from jax.experimental import pallas as pl
from jax.experimental.pallas import tpu as pltpu
from jax.sharding import PartitionSpec as P

NF = 36
ND = 32
LANES = 128
GROUP = 8
MESH = pl.DeviceIdType.MESH


def constants():
    theta = (np.arange(ND) + 0.5) * (2.0 * math.pi / ND)
    freq = 0.04 * np.exp(np.arange(NF) * (math.log(28.0) / (NF - 1)))
    weight = 0.1 * freq * (2.0 * math.pi / ND)
    return np.concatenate([np.cos(theta), np.sin(theta), freq, weight]).astype(np.float32)


def take(x, index):
    return lax.gather(
        x, index[..., None],
        lax.GatherDimensionNumbers((), (1,), (1,), (0,), (0,)),
        (1, 1), mode=lax.GatherScatterMode.PROMISE_IN_BOUNDS,
    )


def take_wide(low, high, column):
    index = column & (LANES - 1)
    return jnp.where(column >= LANES, take(high, index), take(low, index))


def step_kernel(
    tiles, y_count,
    spectrum_hbm, order_hbm, mask_hbm, depth_hbm, wind_hbm, angle_hbm, speed_hbm, friction_hbm, const_hbm, cos_hbm,
    x_ref, p_ref,
    speed_s, friction_s, const_s,
    cos_v, e, order_v, mask_v, depth_v, wind_v, angle_v,
    col_v, water_v, wet_v, inv, nbr, nbr_mask, spd, fri, wx, wy, edge, coef, halo_out, halo_in, rim_out, rim_in, rim_sum, rim_all,
    gain, sent, part, part_in, total, total_in, damp_out, damp,
    ready, passed, in_sem, halo_send, halo_recv, rim_send, rim_recv, r_send, r_recv, a_send, a_recv, b_send, b_recv, c_send, c_recv,
):
    comps = e.shape[0]
    rows, lanes = order_v.shape
    tile = lax.axis_index("tile")
    comp = lax.axis_index("comp")
    q = lax.rem(comp, GROUP)
    y = lax.div(comp, GROUP)
    first = comp * comps
    f0 = lax.div(first, ND)
    f1 = lax.div(first + comps - 1, ND)
    has = (tile < tiles - 1, tile > 0)
    beside = (tile + 1, tile - 1)
    group = [(tile, y * GROUP + lax.rem(q + o, GROUP)) for o in range(GROUP)]
    ring = [(tile, lax.rem(y + o, y_count) * GROUP + q) for o in range(y_count)]
    order_a = sorted(range(1, GROUP), key=lambda o: abs(2 * o - GROUP))
    order_b = sorted(range(1, y_count), key=lambda o: abs(2 * o - y_count))
    inner = slice(8, rows + 8)

    copies = [
        pltpu.make_async_copy(src, dst, in_sem.at[i])
        for i, (src, dst) in enumerate(
            [(order_hbm, order_v), (mask_hbm, mask_v), (depth_hbm, depth_v),
             (wind_hbm, wind_v), (angle_hbm, angle_v), (speed_hbm, speed_s), (friction_hbm, friction_s),
             (const_hbm, const_s), (spectrum_hbm, e.at[:, inner, :]), (cos_hbm, cos_v)]
        )
    ]
    for copy in copies:
        copy.start()

    barrier = pltpu.get_barrier_semaphore()
    for to in [group[o] for o in order_a] + [ring[1], ring[y_count - 1]]:
        pl.semaphore_signal(barrier, inc=1, device_id=to, device_id_type=MESH)
    @pl.when(has[0])
    def _():
        for n in range(GROUP):
            pl.semaphore_signal(barrier, inc=1, device_id=(beside[0], y * GROUP + n), device_id_type=MESH)

    zero8 = jnp.zeros((8, lanes), jnp.float32)
    for rim_rows in (slice(0, 8), slice(rows + 8, rows + 16)):
        inv[rim_rows, :] = jnp.zeros((8, lanes), jnp.int32)
        for k in range(comps):
            e[k, rim_rows, :] = zero8
        for h in range(2):
            spd[h, rim_rows, :] = zero8

    for copy in copies[:3] + copies[5:8]:
        copy.wait()
    sub = lax.broadcasted_iota(jnp.int32, (8, lanes), 0)
    spot = lax.broadcasted_iota(jnp.int32, (8, lanes), 1)
    groups = [slice(8 * n, 8 * n + 8) for n in range(GROUP)]
    inners = [slice(8 * n + 8, 8 * n + 16) for n in range(GROUP)]
    classes = [
        [(speed_s[n, f], friction_s[n, f]) for n in range(8)] for f in (f0, f1)
    ]
    for n, at in enumerate(groups):
        column = order_v[at, :] - (sub + 8 * n) * (2 * lanes)
        index = column & (lanes - 1)
        upper = column >= lanes
        halves = [mask_v[at, h] + 2 * depth_v[at, h] for h in (slice(0, lanes), slice(lanes, 2 * lanes))]
        cell = jnp.where(upper, take(halves[1], index), take(halves[0], index))
        wet = (cell & 1) > 0
        kind = cell >> 1
        water = jnp.where(wet, 1.0, 0.0)
        col_v[at, :] = column
        water_v[at, :] = water
        wet_v[at, :] = jnp.where(wet, column, 4 * lanes)
        s = [jnp.full((8, lanes), c[0][0]) for c in classes]
        r = [jnp.full((8, lanes), c[0][1]) for c in classes]
        for m in range(1, 8):
            here = kind == m
            for i in range(2):
                s[i] = jnp.where(here, classes[i][m][0], s[i])
                r[i] = jnp.where(here, classes[i][m][1], r[i])
        for i in range(2):
            spd[i, inners[n], :] = s[i] * water
            fri[i, at, :] = r[i]

    copies[8].wait()
    gain[...] = jnp.zeros_like(gain)
    for a in range(8):
        for rim_rows in (slice(0, 8), slice(rows + 8, rows + 16)):
            sent[a, rim_rows, :] = zero8

    def gather_up(step, carry):
        for pair in range(3):
            k = 6 * step + 2 * pair
            d = lax.rem(first + k, ND)
            i = lax.div(first + k, ND) - f0
            bx = lax.rem(lax.div(d + 8, 16), 2)
            by = lax.div(d, 16)
            cos = [jnp.abs(const_s[d + u]) for u in range(2)]
            sin = [jnp.abs(const_s[ND + d + u]) for u in range(2)]
            energy = [e[k + u, inner, :] for u in range(2)]
            gain[i] += energy[0] + energy[1]
            gain[2 + 2 * bx + i] += cos[0] * energy[0] + cos[1] * energy[1]
            gain[6 + 2 * by + i] += sin[0] * energy[0] + sin[1] * energy[1]
        return carry

    for step in range(comps // 6):
        gather_up(step, 0)

    narrow = jnp.int16
    lane = lax.broadcasted_iota(jnp.int32, (rows, lanes), 1)
    near = lane.astype(narrow)
    far = (lane + lanes).astype(narrow)
    here = wet_v[...].astype(narrow)
    low = jnp.full((rows, lanes), -1, narrow)
    high = low
    for j in range(lanes):
        turned = here if j == 0 else pltpu.roll(here, j, 1)
        slot = ((lane - j) & (lanes - 1)).astype(narrow)
        low = jnp.where(turned == near, slot, low)
        high = jnp.where(turned == far, slot, high)
    inv[inner, :] = (low.astype(jnp.int32) + 1) | ((high.astype(jnp.int32) + 1) << 8)

    for n, at in enumerate(groups):
        column = col_v[at, :]
        water = water_v[at, :]
        index = column & (lanes - 1)
        upper = column >= lanes
        got = take(inv[8 * n + 7 : 8 * n + 15, :] | (inv[8 * n + 9 : 8 * n + 17, :] << 16), index)
        got = jnp.where(upper, got >> 8, got)
        for b in range(2):
            found = ((got >> 16 if b else got) & 255) - 1
            nbr[b, at, :] = jnp.maximum(found, 0)
            nbr_mask[b, at, :] = jnp.where(found >= 0, water, 0.0)
        for b in range(2):
            shifted = column - 1 + 2 * b
            got = take(inv[inners[n], :], shifted & (lanes - 1))
            found = (jnp.where(shifted >= lanes, got >> 8, got) & 255) - 1
            inside = (shifted >= 0) & (shifted < 2 * lanes) & (found >= 0)
            nbr[2 + b, at, :] = jnp.maximum(found, 0)
            nbr_mask[2 + b, at, :] = jnp.where(inside, water, 0.0)

    w0 = const_s[2 * ND + NF + f0]
    w1 = const_s[2 * ND + NF + f1]
    v0 = w0 * const_s[2 * ND + f0]
    v1 = w1 * const_s[2 * ND + f1]
    for n, at in enumerate(groups):
        speed = [spd[i, inners[n], :] for i in range(2)]
        scale = ((w0 * speed[0], w1 * speed[1]), (v0 * speed[0], v1 * speed[1]))
        water = water_v[at, :]
        plain = [gain[i, at, :] for i in range(2)]
        across = [[gain[2 + 2 * a + i, at, :] for i in range(2)] for a in range(4)]
        for h in range(2):
            side = [scale[h][0] * across[a][0] + scale[h][1] * across[a][1] for a in range(4)]
            weights = ((w0, w1), (v0, v1))[h]
            part[n, h] = water * (weights[0] * plain[0] + weights[1] * plain[1]) - (side[0] + side[1] + side[2] + side[3])
            for a in range(4):
                sent[2 * a + h, inners[n], :] = side[a]
    for n, at in enumerate(groups):
        for a in range(4):
            rows_at = slice(8 * n + 7 + 2 * a, 8 * n + 15 + 2 * a) if a < 2 else inners[n]
            index = nbr[a, at, :]
            mask = nbr_mask[a, at, :]
            for h in range(2):
                part[n, h] += mask * take(sent[2 * a + h, rows_at, :], index)
    for b, at in ((0, rows - 1), (1, 0)):
        packed = inv[8 + at : 9 + at, :]
        back = [(packed & 255) - 1, (packed >> 8) - 1]
        both = jnp.where(lax.rem(sub, 2) == 0, sent[2 * b, 8 + at : 9 + at, :], sent[2 * b + 1, 8 + at : 9 + at, :])
        found = jnp.where(sub < 2, back[0], back[1])
        rim_out[b] = jnp.where(found >= 0, take(both, jnp.maximum(found, 0)), 0.0)

    def halo(b, to):
        return pltpu.make_async_remote_copy(
            src_ref=halo_out.at[b], dst_ref=halo_in.at[b], send_sem=halo_send.at[b], recv_sem=halo_recv.at[b],
            device_id=(to, comp), device_id_type=MESH,
        )

    def rim(b, n):
        return pltpu.make_async_remote_copy(
            src_ref=rim_out.at[b], dst_ref=rim_in.at[b, q], send_sem=rim_send.at[b], recv_sem=rim_recv.at[b],
            device_id=(beside[b], y * GROUP + n), device_id_type=MESH,
        )

    def drain(ref, sem):
        pltpu.make_async_copy(ref, ref, sem).wait()

    def send_beside(b):
        for n in (3, 4, 2, 5, 1, 6, 0, 7):
            rim(b, n).start()

    def relay(step):
        for o in (step + 1, y_count - step - 1):
            pl.semaphore_signal(passed.at[step], inc=1, device_id=ring[o], device_id_type=MESH)

    pl.semaphore_wait(barrier, GROUP + 1 + GROUP * lax.div(tile + tiles - 1, tiles))
    relay(0)
    scatters = {
        o: pltpu.make_async_remote_copy(
            src_ref=part.at[lax.rem(q + o, GROUP)], dst_ref=part_in.at[o - 1], send_sem=a_send, recv_sem=a_recv,
            device_id=group[o], device_id_type=MESH,
        )
        for o in order_a
    }
    for o in order_a:
        scatters[o].start()

    @pl.when(has[1])
    def _():
        for n in range(GROUP):
            pl.semaphore_signal(ready, inc=1, device_id=(beside[1], y * GROUP + n), device_id_type=MESH)
        send_beside(1)

    pl.semaphore_wait(passed.at[0], 2)
    if y_count > 4:
        relay(1)

    copies[9].wait()
    pad = edge.shape[1]
    comp_at = first + lax.broadcasted_iota(jnp.int32, (pad, lanes), 0)
    second = comp_at >= ND * (f0 + 1)
    turn = (((comp_at & (ND - 1)) + 8) >> 4) & 1
    spread = jnp.abs(cos_v[pl.ds(lax.rem(first, ND), pad), :])
    for b in range(2):
        for i in range(2):
            coef[2 * b + i] = jnp.where((turn == b) & (second == (i == 1)), spread, 0.0)
    for b, at in ((0, rows - 1), (1, 0)):
        speed = jnp.where(second, spd[1, 8 + at : 9 + at, :], spd[0, 8 + at : 9 + at, :])
        edge[b, :comps, :] = e[:, 8 + at, :] * speed[:comps]

    for b, at in ((0, rows - 1), (1, 0)):
        packed = inv[8 + at : 9 + at, :]
        for h in range(2):
            found = jnp.broadcast_to((packed >> 8 if h else packed & 255) - 1, (pad, lanes))
            halo_out[b, h] = jnp.where(found >= 0, take(edge[b], jnp.maximum(found, 0)), 0.0)

    @pl.when(has[1])
    def _():
        halo(1, beside[1]).start()

    def advect(step, carry):
        for pair in range(3):
            advect_pair(6 * step + 2 * pair)
        return carry

    def advect_pair(k):
        f = lax.div(first + k, ND)
        d = lax.rem(first + k, ND)
        i = f - f0
        bx = lax.rem(lax.div(d + 8, 16), 2)
        by = lax.div(d, 16)
        cos = [jnp.abs(const_s[d + u]) for u in range(2)]
        sin = [jnp.abs(const_s[ND + d + u]) for u in range(2)]
        for n, at in enumerate(groups):
            speed = spd[i, inners[n], :]
            behind = pl.ds(8 * n + 7 + 2 * bx, 8)
            speed_x = spd[i, behind, :]
            energy = [e[k + u, inners[n], :] for u in range(2)]
            flux = [energy[u] * speed for u in range(2)]
            flux_x = [e[k + u, behind, :] * speed_x for u in range(2)]
            index = nbr[bx, at, :]
            gx = [take(flux_x[u], index) for u in range(2)]
            index = nbr[2 + by, at, :]
            gy = [take(flux[u], index) for u in range(2)]
            mask_x = nbr_mask[bx, at, :]
            mask_y = nbr_mask[2 + by, at, :]
            water = water_v[at, :]
            for u in range(2):
                moved = energy[u] * water - (cos[u] + sin[u]) * flux[u]
                moved = moved + cos[u] * (mask_x * gx[u]) + sin[u] * (mask_y * gy[u])
                p_ref[k + u, at, :] = moved

    lax.fori_loop(0, comps // 6, advect, 0)

    copies[3].wait()
    copies[4].wait()
    for at in groups:
        column = col_v[at, :]
        index = column & (lanes - 1)
        upper = column >= lanes
        wind = 0.05 * jnp.where(upper, take(wind_v[at, lanes:], index), take(wind_v[at, :lanes], index))
        angle = jnp.where(upper, take(angle_v[at, lanes:], index), take(angle_v[at, :lanes], index))
        wx[at, :] = wind * jnp.cos(angle)
        wy[at, :] = wind * jnp.sin(angle)

    drain(part_in, a_recv)
    for h in range(2):
        held = part[q, h]
        for n in range(GROUP - 1):
            held += part_in[n, h]
        total[h] = held

    if y_count > 4:
        pl.semaphore_wait(passed.at[1], 2)
    exchanges = {
        o: pltpu.make_async_remote_copy(
            src_ref=total, dst_ref=total_in.at[o - 1], send_sem=b_send, recv_sem=b_recv,
            device_id=ring[o], device_id_type=MESH,
        )
        for o in order_b
    }
    for o in order_b:
        exchanges[o].start()

    @pl.when(has[0])
    def _():
        pl.semaphore_wait(ready, GROUP)
        send_beside(0)
        halo(0, beside[0]).start()

    for b, at in ((0, 0), (1, rows - 1)):
        @pl.when(has[1 - b])
        def _():
            halo(b, beside[1 - b]).wait_recv()
            column1 = jnp.broadcast_to(col_v[at : at + 1, :], (pad, lanes))
            came = take_wide(halo_in[b, 0], halo_in[b, 1], column1) * water_v[at : at + 1, :]
            came = came * (coef[2 * b] + coef[2 * b + 1])
            for k in range(comps):
                p_ref[k, at : at + 1, :] += came[k : k + 1]

    def sources(step, carry):
        for u in range(3):
            k = step * 3 + u
            f = lax.div(first + k, ND)
            d = lax.rem(first + k, ND)
            freq = const_s[2 * ND + f]
            push = jnp.maximum((freq * const_s[d]) * wx[...] + (freq * const_s[ND + d]) * wy[...] - 0.05, 0.0)
            p_ref[k] = p_ref[k] * jnp.exp(push - fri[f - f0])
        return carry

    lax.fori_loop(0, comps // 3, sources, 0)

    for b in range(2):
        rim_sum[b] = jnp.zeros((8, lanes), jnp.float32)

        @pl.when(has[1 - b])
        def _():
            drain(rim_in.at[b], rim_recv.at[b])
            came = rim_in[b, 0]
            for n in range(1, GROUP):
                came += rim_in[b, n]
            rim_sum[b] = came

    rims = {
        o: pltpu.make_async_remote_copy(
            src_ref=rim_sum, dst_ref=rim_all.at[o - 1], send_sem=r_send, recv_sem=r_recv,
            device_id=ring[o], device_id_type=MESH,
        )
        for o in order_b
    }
    for o in order_b:
        rims[o].start()

    drain(total_in, b_recv)
    a0 = total[0]
    a1 = total[1]
    for n in range(y_count - 1):
        a0 += total_in[n, 0]
        a1 += total_in[n, 1]

    def damping(m0, m1, wet):
        mean = jnp.where(wet, m1 / jnp.where(wet, m0, 1.0), 1.0)
        square = mean * mean
        alpha = m0 * (square * square)
        return 2.0 * alpha * alpha / mean

    outer = lax.div(q, GROUP - 1)
    rim0 = jnp.where(outer == 1, a0[7:8], a0[0:1])
    rim1 = jnp.where(outer == 1, a1[7:8], a1[0:1])
    wet_here = water_v[pl.ds(pl.multiple_of(q * 8, 8), 8), :] > 0
    mine = damping(a0, a1, wet_here)
    damp_out[0] = mine
    damp_out[1] = jnp.where(sub == 0, rim0, rim1)
    gathers = {
        o: pltpu.make_async_remote_copy(
            src_ref=damp_out, dst_ref=damp.at[q], send_sem=c_send, recv_sem=c_recv,
            device_id=group[o], device_id_type=MESH,
        )
        for o in order_a
    }
    for o in order_a:
        gathers[o].start()
    damp[q, 0] = mine
    damp[q, 1] = damp_out[1]
    drain(rim_all, r_recv)
    added = []
    for b, at in ((0, 0), (1, rows - 1)):
        came = rim_sum[b]
        for n in range(y_count - 1):
            came += rim_all[n, b]
        column1 = col_v[at : at + 1, :]
        found = take(came, jnp.broadcast_to(column1 & (lanes - 1), (8, lanes)))
        ours = water_v[at : at + 1, :]
        added.append(jnp.where(column1 >= lanes, found[2:4], found[0:2]) * ours)
    drain(damp.at[pl.ds(0, GROUP - 1)], c_recv)
    factor = [damp[n, 0] for n in range(GROUP)]
    for b, n, at in ((0, 0, 0), (1, GROUP - 1, rows - 1)):
        both = damp[n, 1][0:2] + added[b]
        fixed = damping(both[0:1], both[1:2], water_v[at : at + 1, :] > 0)
        factor[n] = jnp.where(sub == at % 8, fixed, factor[n])
    for n, at in enumerate(groups):
        wx[at, :] = jnp.exp(-const_s[2 * ND + f0] * factor[n])
        wy[at, :] = jnp.exp(-const_s[2 * ND + f1] * factor[n])
    for k in range(0, comps, 2):
        fade = jnp.where(lax.div(first + k, ND) == f0, wx[...], wy[...])
        for u in range(2):
            x_ref[k + u] = p_ref[k + u] * fade

    drain(part_in, a_send)
    drain(total_in, b_send)
    drain(rim_all, r_send)
    drain(damp.at[pl.ds(0, GROUP - 1)], c_send)
    for b in range(2):
        @pl.when(has[b])
        def _():
            drain(rim_in.at[b], rim_send.at[b])
            halo(b, beside[b]).wait_send()


def body(tiles, y_count, spectrum, sea_mask, sea_order, depth_class, wind_speed, wind_angle, speed_table, friction_table):
    comps = spectrum.shape[0]
    rows = sea_mask.shape[0]
    f32, i32 = jnp.float32, jnp.int32
    hbm = pl.BlockSpec(memory_space=pltpu.HBM)
    vmem = pl.BlockSpec(memory_space=pltpu.VMEM)
    grid = (rows, LANES)
    wide = (rows, 2 * LANES)
    pad = -(-comps // 8) * 8
    V, S, D = pltpu.VMEM, pltpu.SMEM, pltpu.SemaphoreType.DMA
    numbers = constants()
    table = jnp.asarray(numbers)
    doubled = jnp.asarray(np.ascontiguousarray(np.broadcast_to(np.tile(numbers[:ND], 2)[:, None], (2 * ND, LANES))))
    operands = (
        spectrum.reshape(comps, rows, LANES), sea_order.reshape(grid), sea_mask, depth_class, wind_speed, wind_angle,
        speed_table, friction_table, table, doubled,
    )
    result = pl.pallas_call(
        functools.partial(step_kernel, tiles, y_count),
        out_shape=jax.ShapeDtypeStruct((comps,) + grid, f32),
        in_specs=[hbm] * 10,
        out_specs=vmem,
        scratch_shapes=[
            V((comps,) + grid, f32),
            S(speed_table.shape, f32), S(friction_table.shape, f32), S(table.shape, f32),
            V(doubled.shape, f32), V((comps, rows + 16, LANES), f32),
            V(grid, i32), V(wide, i32), V(wide, i32), V(wide, f32), V(wide, f32),
            V(grid, i32), V(grid, f32), V(grid, i32), V((rows + 16, LANES), i32), V((4,) + grid, i32), V((4,) + grid, f32),
            V((2, rows + 16, LANES), f32), V((2,) + grid, f32),
            V(grid, f32), V(grid, f32), V((2, pad, LANES), f32), V((4, pad, LANES), f32),
            V((2, 2, pad, LANES), f32), V((2, 2, pad, LANES), f32), V((2, 8, LANES), f32), V((2, GROUP, 8, LANES), f32),
            V((2, 8, LANES), f32), V((y_count - 1, 2, 8, LANES), f32),
            V((10,) + grid, f32), V((8, rows + 16, LANES), f32),
            V((GROUP, 2, 8, LANES), f32), V((GROUP - 1, 2, 8, LANES), f32),
            V((2, 8, LANES), f32), V((y_count - 1, 2, 8, LANES), f32),
            V((2, 8, LANES), f32), V((GROUP, 2, 8, LANES), f32),
            pltpu.SemaphoreType.REGULAR, pltpu.SemaphoreType.REGULAR((2,)), D((10,)), D((2,)), D((2,)), D((2,)), D((2,)), D, D, D, D, D, D, D, D,
        ],
        compiler_params=pltpu.CompilerParams(collective_id=0, has_side_effects=True, vmem_limit_bytes=32 << 20),
        name="wave_step",
    )(*[pltpu.with_memory_space_constraint(z, pltpu.HBM) for z in operands])
    return result.reshape(spectrum.shape)


def solution(mesh):
    return jax.shard_map(
        functools.partial(body, mesh.shape["tile"], mesh.shape["comp"] // GROUP),
        mesh=mesh,
        in_specs=(
            P("comp", "tile", None),
            P("tile", None),
            P("tile", None),
            P("tile", None),
            P("tile", None),
            P("tile", None),
            P(),
            P(),
        ),
        out_specs=P("comp", "tile", None),
        check_vma=False,
    )
```
